32 devices in a mesh: seq: 8 (over y, x, core), dp: 4 (over z).
Axes of the slice: x: 2, y: 2, z: 4, core: 2. Of those that a mesh axis runs over, the one named last changes fastest.
Arguments:
- queries: bfloat16 [4096, 512], P('seq', 'dp'), may hold values from -40 to 40
- keys: bfloat16 [4096, 512], P('seq', 'dp'), may hold values from -40 to 40
- values: bfloat16 [4096, 512], P('seq', 'dp'), may hold values from -6 to 6
- cross_queries: bfloat16 [4096, 512], P('seq', 'dp'), may hold values from -90 to 90
- encoded: bfloat16 [64, 128, 896], P('dp'), may hold values from -6 to 6
- cross_kv_weight: bfloat16 [896, 2, 512], P(None, None, 'dp'), may hold values from -0.1875 to 0.1875
- owners: int32 [64, 2], P('seq'), may hold values from 0 to 3, all different within a row; in each aligned block of 8 rows (0 to 7, 8 to 15, ...) at most 8 rows name the same one
- tile_rows: int32 [64, 2], P('seq'), may hold values from 0 to 15
Outputs:
- attended: bfloat16 [4096, 512], P('seq', 'dp')
- crossed: bfloat16 [4096, 512], P('seq', 'dp')
The draws below stay inside these ranges and needn't reach their ends.
Inputs may be any that keep to these rules, and one draw needn't show every extreme that they name: `owners`: the 2 entries of a row differ; in each aligned block of 8 rows (the spans of one seq index) no owner is named by more than 8 rows, a bound that some block reaches.
All inputs are finite; a program needn't handle non-finite values.
Results may differ from the reference program's by a relative error of at most 0.0083.
Values may be sent and summed in bfloat16 or wider, within the bound.
A program may use at most 128 MiB of HBM per device.

```python
import math
import jax
import jax.numpy as jnp
import numpy as np
from jax import lax

CL = 64
NB = 2
RL = 128
HS = 128
ENC = 896
POOL_DEV = 16
HEADS = 4
LEN = 4096
SPANS = 64
SPANS_DEV = 8
POOL = 64
CAP = 8
N_DP = 4


def paired_draw(key):
    base = jax.random.fold_in(key, 11)
    key_query, key_key = jax.random.split(base, 2)
    shape = (LEN, HEADS * HS)
    query_part = jnp.clip(1.7 * jax.random.normal(key_query, shape, jnp.float32), -6.8, 6.8)
    key_part = jnp.clip(1.7 * jax.random.normal(key_key, shape, jnp.float32), -6.8, 6.8)
    return (query_part, key_part)


def draw_queries(key, part):
    return paired_draw(key)[0].astype(jnp.bfloat16)


def draw_keys(key, part):
    return paired_draw(key)[1].astype(jnp.bfloat16)


def draw_cross_queries(key, part):
    base = jax.random.fold_in(key, 23)
    shape = (LEN, HEADS * HS)
    sample = jnp.clip(1.7 * jax.random.normal(base, shape, jnp.float32), -6.8, 6.8)
    return sample.astype(jnp.bfloat16)


def set_ends(entries, rng, least, largest):
    longest = entries.shape.index(max(entries.shape))
    spots = []
    for shift in (0, 1):
        where = [jax.random.randint(jax.random.fold_in(rng, axis), (), 0, length) for axis, length in enumerate(entries.shape)]
        where[longest] = (where[longest] + shift) % entries.shape[longest]
        spots.append(tuple(where))
    return entries.at[spots[0]].set(least).at[spots[1]].set(largest)


def steps_of(key, extent, cuts, smallest, top_value):
    factor_of, own = 1.0, jax.random.fold_in(key, 6)
    for axis_at, shards_of in cuts:
        steps = jnp.exp(jax.random.uniform(jax.random.fold_in(own, axis_at), (shards_of,), jnp.float32, smallest / len(cuts), top_value / len(cuts)))
        factor_of = factor_of * jnp.repeat(steps, extent[axis_at] // shards_of).reshape([-1 if axis == axis_at else 1 for axis in range(len(extent))])
    return factor_of


def shared_out(rng, own, number, rows, count, top, reach, slope):
    order = jax.random.permutation(rng, count)
    crowded, usual = portions_of(count, rows * top, reach, slope, True), portions_of(count, rows * top, reach, slope, False)
    places = jnp.arange(count)

    def named(tallies, offset_by):
        used = int((tallies > 0).sum())
        fixed = max(1, used // 4)
        shifted = fixed + (places - fixed + offset_by * (used - fixed)) % max(1, count - fixed)
        return jnp.zeros((count,), jnp.int32).at[order[jnp.where(places < fixed, places, shifted)]].set(jnp.asarray(tallies, jnp.int32))

    tallies = jnp.where(number % 4 == 0, named(crowded, number // 4), named(usual, number - number // 4 - 1))
    mixed = jax.random.permutation(jax.random.fold_in(own, 3), count)
    donor, sink = mixed[0:count // 2 * 2:2], mixed[1:count // 2 * 2:2]
    room = jnp.minimum(tallies[donor] - 1, reach - tallies[sink]) // 2
    room = jnp.where((donor == order[0]) | (sink == order[0]) | (tallies[sink] == 0), 0, jnp.maximum(room, 0))
    shifted = jax.random.randint(jax.random.fold_in(own, 4), (count // 2,), 0, 1 << 20) % (room + 1)
    tallies = tallies.at[donor].add(-shifted).at[sink].add(shifted)
    items = jnp.searchsorted(jnp.cumsum(tallies), jnp.arange(rows * top), side="right").astype(jnp.int32)
    grid = items.reshape(top, rows).T
    grid = grid[jax.random.permutation(jax.random.fold_in(own, 1), rows)]
    offset_by = jax.random.randint(jax.random.fold_in(own, 2), (rows, 1), 0, top)
    return jnp.take_along_axis(grid, (jnp.arange(top)[None, :] + offset_by) % top, axis=1)


def portions_of(amount, total, reach, lean, full):
    weights = [(1 << 20) // math.isqrt(rank ** lean) + 1 for rank in range(1, amount + 1)]
    largest = reach if full else min(reach, max(-(-total // amount), total * weights[0] // sum(weights)))
    least = 1 if total - largest >= amount - 1 else 0
    counts, surplus = [largest] + [least] * (amount - 1), total - largest - least * (amount - 1)
    while surplus > 0:
        free = [i for i in range(1, amount) if counts[i] < largest] or [i for i in range(1, amount) if counts[i] < reach]
        whole, left = sum([weights[i] for i in free]), surplus
        for i in free:
            more = min(reach - counts[i], max(1, left * weights[i] // whole), surplus)
            counts[i] = counts[i] + more
            surplus = surplus - more
    return np.array(counts)


def noise(key, dims, deviation, reach, pieces=(), held_as=jnp.bfloat16):
    drawn = jax.random.normal(key, dims, jnp.float32) * deviation
    if len(pieces) > 0:
        drawn = steps_of(key, dims, pieces, -0.22, 0.18) * drawn
    return jnp.clip(drawn, min=-reach, max=reach).astype(held_as)


def setup_inputs(seed: int = 0) -> dict:
    key_of = jax.random.split(jax.random.key(seed), 9)
    queries = draw_queries(jax.random.fold_in(key_of[8], 71), 0)
    keys = draw_keys(jax.random.fold_in(key_of[8], 71), 0)
    values = noise(key_of[2], (LEN, HEADS * HS), 1.0, 6.0, ((0, 8), (1, 4)))
    cross_queries = draw_cross_queries(jax.random.fold_in(key_of[8], 71), 0)
    encoded = noise(key_of[4], (POOL, RL, ENC), 1.0, 6.0, ((0, 4),))
    cross_kv_weight = noise(key_of[5], (ENC, 2, HEADS * HS), ENC ** -0.5, 0.1875, ((2, 4),))
    owners_keys = jax.random.split(jax.random.fold_in(key_of[6], 1), SPANS // SPANS_DEV)
    owners_turns = jax.random.permutation(jax.random.fold_in(key_of[6], 3), SPANS // SPANS_DEV)
    owners = jax.vmap(lambda own, number: shared_out(jax.random.fold_in(key_of[6], 2), own, number, SPANS_DEV, N_DP, NB, CAP, 2))(owners_keys, owners_turns).reshape((SPANS, NB))
    tile_rows = set_ends(jax.random.randint(key_of[7], (SPANS, NB), 0, POOL_DEV), jax.random.fold_in(key_of[7], 1), 0, POOL_DEV - 1).astype(jnp.int32)
    return {"queries": queries, "keys": keys, "values": values, "cross_queries": cross_queries, "encoded": encoded, "cross_kv_weight": cross_kv_weight, "owners": owners, "tile_rows": tile_rows}


def self_head(head_arrays):
    query_head, key_head, value_head = head_arrays
    block_rows = math.gcd(LEN, 512)
    query_blocks = query_head.reshape(LEN // block_rows, block_rows, HS)
    starts = jnp.arange(LEN // block_rows, dtype=jnp.int32) * block_rows
    inv_root = 1.0 / math.sqrt(HS)
    key_positions = jnp.arange(LEN, dtype=jnp.int32)

    def one_block(item):
        query_block, first_row = item
        scores = jnp.dot(query_block, key_head.T, preferred_element_type=jnp.float32) * inv_root
        positions = first_row + jnp.arange(block_rows, dtype=jnp.int32)
        allowed = key_positions[None, :] <= positions[:, None]
        scores = jnp.where(allowed, scores, jnp.float32(-1e+30))
        row_max = lax.optimization_barrier(jnp.max(scores, axis=1, keepdims=True))
        expo = jnp.where(allowed, jnp.exp(scores - row_max), jnp.float32(0.0))
        total = lax.optimization_barrier(jnp.sum(expo, axis=1, keepdims=True))
        weights = expo.astype(jnp.bfloat16)
        summed = jnp.dot(weights, value_head, preferred_element_type=jnp.float32)
        return (summed / total).astype(jnp.bfloat16)
    return lax.map(one_block, (query_blocks, starts)).reshape(LEN, HS)

def reference(queries, keys, values, cross_queries, encoded, cross_kv_weight, owners, tile_rows):
    width = HEADS * HS
    inv_root = 1.0 / math.sqrt(HS)
    query_heads = queries.reshape(LEN, HEADS, HS).transpose(1, 0, 2)
    key_heads = keys.reshape(LEN, HEADS, HS).transpose(1, 0, 2)
    value_heads = values.reshape(LEN, HEADS, HS).transpose(1, 0, 2)
    head_outs = lax.map(self_head, (query_heads, key_heads, value_heads))
    attended = head_outs.transpose(1, 0, 2).reshape(LEN, width)
    tile_index = (owners * POOL_DEV + tile_rows).astype(jnp.int32)
    padded = jnp.concatenate([cross_queries[CL - 1:], jnp.zeros((CL - 1, width), jnp.bfloat16)], axis=0)
    span_queries = padded.reshape(SPANS, CL, HEADS, HS)
    flat_weight = cross_kv_weight.reshape(ENC, 2 * width)

    def one_span(item):
        query_block, indices = item
        tiles = jnp.take(encoded, indices, axis=0).reshape(NB * RL, ENC)
        projected = jnp.dot(tiles, flat_weight, preferred_element_type=jnp.float32).astype(jnp.bfloat16)
        projected = projected.reshape(NB * RL, 2, HEADS, HS)
        cross_keys = projected[:, 0]
        cross_values = projected[:, 1]
        scores = jnp.einsum('qhd,khd->hqk', query_block.astype(jnp.float32), cross_keys.astype(jnp.float32)) * inv_root
        row_max = lax.optimization_barrier(jnp.max(scores, axis=2, keepdims=True))
        expo = jnp.exp(scores - row_max)
        total = lax.optimization_barrier(jnp.sum(expo, axis=2))
        weights = expo.astype(jnp.bfloat16)
        summed = jnp.einsum('hqk,khd->qhd', weights.astype(jnp.float32), cross_values.astype(jnp.float32))
        result = summed / jnp.transpose(total)[:, :, None]
        return result.reshape(CL, width).astype(jnp.bfloat16)
    span_outs = lax.map(one_span, (span_queries, tile_index)).reshape(LEN, width)
    crossed = jnp.concatenate([jnp.zeros((CL - 1, width), jnp.bfloat16), span_outs[:LEN - CL + 1]], axis=0)
    return (attended, crossed)
```

```python
import functools
import math

import jax
import jax.numpy as jnp
from jax import lax
from jax.experimental import pallas as pl
from jax.experimental.pallas import tpu as pltpu
from jax.sharding import PartitionSpec as P

HS = 128
NEG = -1e30
LOG2E = math.log2(math.e)
MESH = pl.DeviceIdType.MESH
PARTS = 3


def kernel(
    S, D, inv_root,
    own_s, row_s, own_h, row_h, q_h, key_h, val_h, cq_h, enc_h, w_h,
    att, crs,
    prev_v, prev_s, q, cqr, wraw, w32, encv, wall, esel, kvs, cqs,
    acc_st, st, rin, rin_st, rout, fa, fb,
    kall, vall, m_ref, l_ref, acc_ref,
    lsem, id_send, id_recv, id_sem,
    sw, rw, sws, rws, scq, rcq, sra, rra, srs, rrs,
    send_k, recv_k, send_r, send_ks, recv_ks,
):
    f32, bf = jnp.float32, jnp.bfloat16
    s = lax.axis_index("seq")
    d = lax.axis_index("dp")
    k = s % 2
    g = s // 2
    c = g % 4
    base = g - c
    chips = S // 2
    sib = s + 1 - 2 * k
    nxt = (s + 1) % S
    prv = (s + S - 1) % S
    T = q.shape[0]
    near, spans_here = own_s.shape
    slots = spans_here + 1
    span_len = T // spans_here
    tile_len = encv.shape[1]
    wide = encv.shape[2]
    quarter = wide // 4
    R = cqs.shape[1]
    tail = R - T
    groups = span_len // tail
    lane_step = HS // groups
    half_step = lane_step // 2
    scale = inv_root * LOG2E

    def sq(chip):
        return {"seq": chip * 2 + k}

    bar = pltpu.get_barrier_semaphore()

    def greet(to):
        pl.semaphore_signal(bar, 1, device_id=to, device_id_type=MESH)

    greet({"seq": sib})
    greet(sq(base + (c + 1 - 2 * (c % 2))))
    greet(sq(base + (c + 2) % 4))

    @pl.when(k == 1)
    def _():
        greet({"seq": nxt})

    @pl.when(k == 0)
    def _():
        greet({"seq": prv})

    @pl.when(d > 0)
    def _():
        greet({"dp": d - 1})

    @pl.when(d + 1 < D)
    def _():
        greet({"dp": d + 1})

    @pl.loop(4, chips)
    def _(o):
        greet(sq((base + o) % chips))

    wcopy = pltpu.make_async_copy(w_h, wraw, lsem.at[0])
    kcopy = pltpu.make_async_copy(key_h, kall.at[s], lsem.at[1])
    vcopy = pltpu.make_async_copy(val_h, vall.at[s], lsem.at[2])
    ccopy = pltpu.make_async_copy(cq_h, cqr, lsem.at[3])
    qcopy = pltpu.make_async_copy(q_h, q, lsem.at[4])
    ecopy = pltpu.make_async_copy(enc_h, encv, lsem.at[5])
    for cp in (wcopy, kcopy, vcopy, ccopy, qcopy, ecopy):
        cp.start()

    wcopy.wait()
    w32[...] = wraw[...].astype(f32)
    for kv in range(2):
        wall[d, kv] = w32[pl.ds(kv, wide, stride=2), :].astype(bf)

    ccopy.wait()
    shifted = jnp.concatenate([cqr[...].astype(f32), jnp.zeros((tail, HS), f32)], axis=0)
    cqs[d] = pltpu.roll(shifted, 1, 0).astype(bf)
    kcopy.wait()
    vcopy.wait()

    def id_copy(i, ref):
        return pltpu.make_async_remote_copy(
            ref, prev_v.at[i], id_send.at[i], id_recv.at[i], device_id={"seq": nxt}, device_id_type=MESH)

    def w_copy(h, cc, to, sem):
        ref = wall.at[h, k, pl.ds(cc * quarter, quarter)]
        return pltpu.make_async_remote_copy(ref, ref, sem, rw.at[h, cc], device_id=to, device_id_type=MESH)

    xc = c + 1 - 2 * (c % 2)
    yc = (c + 2) % 4
    dc = 3 - c
    x_to, y_to = sq(base + xc), sq(base + yc)

    def w_z(h, dirn):
        return w_copy(h, c, {"dp": d + dirn}, sw.at[h, 0 if dirn < 0 else 1])

    def w_x(h):
        return w_copy(h, c, x_to, sw.at[h, 2])

    def w_y(h):
        return w_copy(h, c, y_to, sw.at[h, 3])

    def w_relay0(h):
        return w_copy(h, xc, y_to, sw.at[h, 4])

    def w_relay1(h):
        return w_copy(h, yc, x_to, sw.at[h, 4])

    def w_recv(h, cc):
        w_copy(h, cc, {"seq": sib}, rw.at[h, cc]).wait_recv()

    def w_sib(h, cc, kk):
        ref = wall.at[h, kk, pl.ds(cc * quarter, quarter)]
        return pltpu.make_async_remote_copy(
            ref, ref, sws.at[h, cc], rws.at[h, cc], device_id={"seq": sib}, device_id_type=MESH)

    def cq_copy(h, dirn):
        return pltpu.make_async_remote_copy(
            cqs.at[h], cqs.at[h], scq.at[h, 0 if dirn < 0 else 1], rcq.at[h],
            device_id={"dp": d + dirn}, device_id_type=MESH)

    parts = ((0, kall), (1, vall))

    def kv_copy(i, land, src, to, sem):
        ref = land.at[src * 2 + k]
        return pltpu.make_async_remote_copy(
            ref, ref, sem, recv_k.at[i, src], device_id=sq(to), device_id_type=MESH)

    def kv_recv(i, land, src):
        kv_copy(i, land, src, (g + 1) % chips, recv_k.at[i, src]).wait_recv()

    def kv_sib(i, land, src, kk):
        ref = land.at[src * 2 + kk]
        return pltpu.make_async_remote_copy(
            ref, ref, send_ks.at[i, src], recv_ks.at[i, src], device_id={"seq": sib}, device_id_type=MESH)

    def kv_own(what):
        @pl.when(c == 0)
        def _():
            for i, land in parts:
                what(kv_copy(i, land, g, base + 1, send_k.at[i, base + 1]))
                what(kv_copy(i, land, g, base + 2, send_k.at[i, base + 2]))

        @pl.when((c == 1) | (c == 2))
        def _():
            for i, land in parts:
                what(kv_copy(i, land, g, base + 3, send_k.at[i, base + 3]))

        @pl.loop(base + 4, chips)
        def _(to):
            for i, land in parts:
                what(kv_copy(i, land, g, to, send_k.at[i, to]))

        @pl.when(k == 0)
        def _():
            for i, land in parts:
                what(kv_sib(i, land, g, 0))

    def kv_relay(i, land, src, what):
        @pl.when((c == i + 1) & (src == base))
        def _():
            what(kv_copy(i, land, src, base + 3, send_r.at[i, src]))

        @pl.when((c == 3) & (src == base + 1))
        def _():
            what(kv_copy(i, land, src, base + 2, send_r.at[i, src]))

    dirs = (1, -1)

    def valid(h):
        return (h >= 0) & (h < D)

    pl.semaphore_wait(
        bar, 4 + (chips - 4) + jnp.where(d > 0, 1, 0) + jnp.where(d + 1 < D, 1, 0))

    for dirn in dirs:
        @pl.when(valid(d + dirn))
        def _():
            w_z(d, dirn).start()

    for i, ref in ((0, own_h), (1, row_h)):
        id_copy(i, ref).start()

    half = T // 2

    qcopy.wait()
    for h in range(2):
        rows = pl.ds(h * half, half)
        sc = lax.dot_general(q[rows, :], kall[s], (((1,), (1,)), ((), ())),
                             preferred_element_type=f32) * scale
        r = lax.broadcasted_iota(jnp.int32, sc.shape, 0) + h * half
        cc = lax.broadcasted_iota(jnp.int32, sc.shape, 1)
        sc = jnp.where(cc <= r, sc, NEG)
        mx = jnp.max(sc, axis=1, keepdims=True)
        ex = jnp.exp2(sc - mx)
        m_ref[rows, :] = mx
        l_ref[rows, :] = jnp.sum(ex, axis=1, keepdims=True)
        acc_ref[rows, :] = jnp.dot(ex.astype(bf), vall[s], preferred_element_type=f32)

    def attend(b):
        for h in range(2):
            rows = pl.ds(h * half, half)
            sc = lax.dot_general(q[rows, :], kall[b], (((1,), (1,)), ((), ())),
                                 preferred_element_type=f32) * scale
            old = m_ref[rows, :]
            mx = jnp.maximum(old, jnp.max(sc, axis=1, keepdims=True))
            ex = jnp.exp2(sc - mx)
            fade = jnp.exp2(old - mx)
            m_ref[rows, :] = mx
            l_ref[rows, :] = l_ref[rows, :] * fade + jnp.sum(ex, axis=1, keepdims=True)
            acc_ref[rows, :] = acc_ref[rows, :] * fade + jnp.dot(
                ex.astype(bf), vall[b], preferred_element_type=f32)

    def find(owner_of, row_of):
        row, named = row_of(0), owner_of(0) == d
        for n in range(1, near):
            mine = owner_of(n) == d
            row = jnp.where(mine, row_of(n), row)
            named = named | mine
        return row, named

    def slot_at(j):
        if j == 0:
            return find(lambda n: prev_s[0, n, spans_here - 1], lambda n: prev_s[1, n, spans_here - 1])
        return find(lambda n: own_s[n, j - 1], lambda n: row_s[n, j - 1])

    def pick(j):
        row, _ = slot_at(j)
        esel[j * tile_len:(j + 1) * tile_len, :] = encv[row]

    lane = lax.broadcasted_iota(jnp.int32, (span_len, HS), 1)
    per = -(-slots // PARTS)
    chunks = [range(a, min(a + per, slots)) for a in range(0, slots, per)]

    def rows_of(js):
        a = js[0] * span_len
        b = R if js[-1] == slots - 1 else (js[-1] + 1) * span_len
        return slice(a, b)

    def compute(h):
        weight = jnp.concatenate([wall[h, 0], wall[h, 1]], axis=1)
        for js in chunks:
            part = pl.ds(js[0] * tile_len, len(js) * tile_len)
            kvs[part, :] = jnp.dot(esel[part, :], weight, preferred_element_type=f32).astype(bf)
        packed = jnp.zeros((span_len, HS), f32)
        for j in range(slots):
            _, named = slot_at(j)
            rows = rows_of([j])
            n = rows.stop - rows.start
            kv = kvs[j * tile_len:(j + 1) * tile_len, :]
            sc = lax.dot_general(cqs[h, rows, :], kv[:, :HS], (((1,), (1,)), ((), ())),
                                 preferred_element_type=f32) * scale
            mx = jnp.max(sc, axis=1, keepdims=True)
            ex = jnp.exp2(sc - mx)
            tot = jnp.sum(ex, axis=1, keepdims=True)
            out = jnp.dot(ex.astype(bf), kv[:, HS:], preferred_element_type=f32)
            acc_st[h, rows, :] = jnp.where(named, out, 0.0)
            mx = jnp.where(named, mx, NEG)
            tot = jnp.where(named, tot, 0.0)
            if n < span_len:
                rest = jnp.zeros((span_len - n, 1), f32)
                mx = jnp.concatenate([mx, rest], axis=0)
                tot = jnp.concatenate([tot, rest], axis=0)
            packed = jnp.where(lane == j, mx, packed)
            packed = jnp.where(lane == half_step + j, tot, packed)
        st[h] = sum(
            [packed[r * tail:(r + 1) * tail] if r == 0
             else pltpu.roll(packed[r * tail:(r + 1) * tail], r * lane_step, 1) for r in range(groups)])

    def unpack(x):
        return jnp.concatenate(
            [x if r == 0 else pltpu.roll(x, HS - r * lane_step, 1) for r in range(groups)], axis=0)

    def ret_copy(h, ch, slot, to):
        a = rows_of(chunks[ch])
        part = pl.ds(a.start, a.stop - a.start)
        return pltpu.make_async_remote_copy(
            rout.at[h, part], rin.at[slot, part], sra.at[h, ch], rra.at[slot, ch],
            device_id={"dp": to}, device_id_type=MESH)

    def st_copy(h, slot, to):
        return pltpu.make_async_remote_copy(
            st.at[h], rin_st.at[slot], srs.at[h], rrs.at[slot],
            device_id={"dp": to}, device_id_type=MESH)

    def way(h):
        to = jnp.where(h > d, d + 1, d - 1)
        slot = jnp.where(to == h, jnp.where(h > d, D, D + 1), h)
        return jnp.clip(to, 0, D - 1), slot

    packed_lane = lax.broadcasted_iota(jnp.int32, (tail, HS), 1) % lane_step

    def ship(h, slot_in, incoming, send):
        to, slot = way(h)
        other = jnp.where(d > 0, d - 1, d + 1)

        @pl.when(incoming)
        def _():
            st_copy(h, slot_in, other).wait_recv()
            a, b = st[h], rin_st[slot_in]
            top = jnp.maximum(a, b)
            fade_a, fade_b = jnp.exp2(a - top), jnp.exp2(b - top)
            tot = (fade_a * pltpu.roll(a, HS - half_step, 1)
                   + fade_b * pltpu.roll(b, HS - half_step, 1))
            st[h] = jnp.where(packed_lane < half_step, top, pltpu.roll(tot, half_step, 1))
            fa[...] = unpack(fade_a)
            fb[...] = unpack(fade_b)

        @pl.when(send)
        def _():
            st_copy(h, slot, to).start()

        for ch, js in enumerate(chunks):
            @pl.when(incoming)
            def _():
                ret_copy(h, ch, slot_in, other).wait_recv()
                for j in js:
                    rows = rows_of([j])
                    n = rows.stop - rows.start
                    acc_st[h, rows, :] = (fa[:n, j:j + 1] * acc_st[h, rows, :]
                                          + fb[:n, j:j + 1] * rin[slot_in, rows, :].astype(f32))

            @pl.when(send)
            def _():
                rows = rows_of(js)
                rout[h, rows, :] = acc_st[h, rows, :].astype(bf)
                ret_copy(h, ch, slot, to).start()

    at_end = (d == 0) | (d == D - 1)

    ecopy.wait()
    for j in range(1, slots):
        pick(j)

    for i, ref in ((0, own_h), (1, row_h)):
        id_copy(i, ref).wait_recv()
        pltpu.make_async_copy(prev_v.at[i], prev_s.at[i], id_sem.at[i]).start()
    for i in range(2):
        pltpu.make_async_copy(prev_v.at[i], prev_s.at[i], id_sem.at[i]).wait()
    pick(0)

    def kv_stage(src):
        for i, land in parts:
            kv_recv(i, land, src)
            kv_relay(i, land, src, lambda cp: cp.start())
            kv_sib(i, land, src, k).start()

    def kv_done(src):
        for i, land in parts:
            kv_sib(i, land, src, 1 - k).wait_recv()
        attend(src * 2)
        attend(src * 2 + 1)

    def order(i):
        return base + jnp.where(c == 3, (i + 1) % 3, i)

    @pl.loop(1, D + 3)
    def _(e):
        for dirn in dirs:
            h = d - dirn * e

            @pl.when((e < D) & valid(h))
            def _():
                w_recv(h, c)

                @pl.when(valid(d + dirn))
                def _():
                    w_z(h, dirn).start()

                w_x(h).start()
                w_y(h).start()
                w_sib(h, c, k).start()

        @pl.when(e == 1)
        def _():
            for dirn in dirs:
                @pl.when(valid(d + dirn))
                def _():
                    cq_copy(d, dirn).start()

            kv_own(lambda cp: cp.start())

        for dirn in dirs:
            h = d - dirn * (e - 1)

            @pl.when((e > 1) & (e <= D) & valid(h))
            def _():
                w_recv(h, xc)

                @pl.when(k == 0)
                def _():
                    w_relay0(h).start()

                w_sib(h, xc, k).start()
                w_recv(h, yc)

                @pl.when(k == 1)
                def _():
                    w_relay1(h).start()

                w_sib(h, yc, k).start()

                cq_copy(h, dirn).wait_recv()

                @pl.when(valid(d + dirn))
                def _():
                    cq_copy(h, dirn).start()

        for dirn in dirs:
            h = d - dirn * (e - 2)

            @pl.when((e > 2) & (e <= D + 1) & valid(h))
            def _():
                w_recv(h, dc)
                w_sib(h, dc, k).start()

        @pl.when(e == 1)
        def _():
            compute(d)

        @pl.when(e == D)
        def _():
            @pl.when(k == 1)
            def _():
                for i, land in parts:
                    kv_sib(i, land, g, 0).wait_recv()
                attend(s - 1)

        @pl.when(e > 3)
        def _():
            @pl.loop(0, 2)
            def _(side):
                h = d + (2 * side - 1) * (e - 3)

                @pl.when(valid(h))
                def _():
                    for cc in range(4):
                        w_sib(h, cc, 1 - k).wait_recv()
                    compute(h)

                    @pl.when(at_end)
                    def _():
                        ship(h, h, False, True)

    @pl.loop(0, base)
    def _(src):
        kv_stage(src)
        kv_done(src)

    @pl.loop(0, c)
    def _(i):
        kv_stage(order(i))

    right_first = 2 * d < D - 1
    first = jnp.where(right_first, D - 1 - d, d)
    sgn = jnp.where(right_first, 1, -1)

    @pl.loop(0, D + 1)
    def _(i):
        h = jnp.where(i < first, d + sgn * (i + 1), d - sgn * (i - first + 1))
        last = i >= D - 1
        h = jnp.where(last, d, h)
        slot = jnp.where(last, i + 1, h)
        through = jnp.logical_not(last) & jnp.logical_not(at_end)
        final = ((i == D - 1) & (d > 0)) | ((i == D) & (d + 1 < D))

        @pl.when(i == D - 1)
        def _():
            @pl.loop(0, c)
            def _(i):
                kv_done(order(i))

        @pl.when(through | final)
        def _():
            ship(h, slot, True, through)

    att[...] = (acc_ref[...] / l_ref[...]).astype(bf)

    tots = unpack(pltpu.roll(st[d], HS - half_step, 1))
    for j in range(slots):
        rows = rows_of([j])
        n = rows.stop - rows.start
        out = acc_st[d, rows, :] / tots[:n, j:j + 1]
        if j == 0:
            out = jnp.where(s > 0, out, 0.0)
        acc_st[d, rows, :] = out
    crs[...] = pltpu.roll(acc_st[d], R - 1, 0)[:T].astype(bf)

    for i, ref in ((0, own_h), (1, row_h)):
        id_copy(i, ref).wait_send()

    for dirn in dirs:
        @pl.when(valid(d + dirn))
        def _():
            w_z(d, dirn).wait_send()
            cq_copy(d, dirn).wait_send()

        @pl.loop(1, D)
        def _(e):
            h = d - dirn * e

            @pl.when(valid(h))
            def _():
                @pl.when(valid(d + dirn))
                def _():
                    w_z(h, dirn).wait_send()
                    cq_copy(h, dirn).wait_send()

                w_x(h).wait_send()
                w_y(h).wait_send()
                w_relay0(h).wait_send()
                for cc in range(4):
                    w_sib(h, cc, k).wait_send()
                to, slot = way(h)
                st_copy(h, slot, to).wait_send()
                for ch in range(len(chunks)):
                    ret_copy(h, ch, slot, to).wait_send()

    kv_own(lambda cp: cp.wait_send())

    @pl.loop(0, g)
    def _(src):
        for i, land in parts:
            kv_relay(i, land, src, lambda cp: cp.wait_send())
            kv_sib(i, land, src, k).wait_send()


def on_device(queries, keys, values, cross_queries, encoded, cross_kv_weight, owners, tile_rows):
    S, D = lax.axis_size("seq"), lax.axis_size("dp")
    T, width = queries.shape
    pool_here, tile_len, wide = encoded.shape
    spans_here = owners.shape[0]
    slots = spans_here + 1
    span_len = T // spans_here
    R = T + 16
    w = cross_kv_weight.reshape(2 * wide, HS)
    own, row = owners.T, tile_rows.T
    near = own.shape[0]
    chips = S // 2
    nc = -(-slots // -(-slots // PARTS))
    bf, f32 = jnp.bfloat16, jnp.float32
    vm = pl.BlockSpec(memory_space=pltpu.VMEM)
    hbm = pl.BlockSpec(memory_space=pl.ANY)
    dma = pltpu.SemaphoreType.DMA
    attended, crossed = pl.pallas_call(
        functools.partial(kernel, S, D, 1.0 / math.sqrt(HS)),
        name="retro",
        out_shape=(jax.ShapeDtypeStruct((T, width), bf), jax.ShapeDtypeStruct((T, width), bf)),
        in_specs=[pl.BlockSpec(memory_space=pltpu.SMEM)] * 2 + [hbm] * 8,
        out_specs=(vm, vm),
        scratch_shapes=[
            pltpu.VMEM((2, near, spans_here), jnp.int32),
            pltpu.SMEM((2, near, spans_here), jnp.int32),
            pltpu.VMEM((T, HS), bf),
            pltpu.VMEM((T, HS), bf),
            pltpu.VMEM((2 * wide, HS), bf),
            pltpu.VMEM((2 * wide, HS), f32),
            pltpu.VMEM((pool_here, tile_len, wide), bf),
            pltpu.VMEM((D, 2, wide, HS), bf),
            pltpu.VMEM((slots * tile_len, wide), bf),
            pltpu.VMEM((slots * tile_len, 2 * HS), bf),
            pltpu.VMEM((D, R, HS), bf),
            pltpu.VMEM((D, R, HS), f32),
            pltpu.VMEM((D, 16, HS), f32),
            pltpu.VMEM((D + 2, R, HS), bf),
            pltpu.VMEM((D + 2, 16, HS), f32),
            pltpu.VMEM((D, R, HS), bf),
            pltpu.VMEM((span_len, HS), f32),
            pltpu.VMEM((span_len, HS), f32),
            pltpu.VMEM((S, T, HS), bf),
            pltpu.VMEM((S, T, HS), bf),
            pltpu.VMEM((T, 1), f32),
            pltpu.VMEM((T, 1), f32),
            pltpu.VMEM((T, HS), f32),
            dma((6,)), dma((2,)), dma((2,)), dma((2,)),
            dma((D, 5)), dma((D, 4)), dma((D, 4)), dma((D, 4)), dma((D, 2)), dma((D,)),
            dma((D, nc)), dma((D + 2, nc)), dma((D,)), dma((D + 2,)),
            dma((2, chips)), dma((2, chips)), dma((2, chips)), dma((2, chips)), dma((2, chips)),
        ],
        compiler_params=pltpu.CompilerParams(
            collective_id=0, has_side_effects=True, vmem_limit_bytes=60 * 1024 * 1024),
    )(own, row, own, row, queries, keys, values, cross_queries, encoded, w)
    return attended, crossed


def solution(mesh):
    placed = (
        P("seq", "dp"),
        P("seq", "dp"),
        P("seq", "dp"),
        P("seq", "dp"),
        P("dp", None, None),
        P(None, None, "dp"),
        P("seq", None),
        P("seq", None),
    )
    return jax.shard_map(
        on_device,
        mesh=mesh,
        in_specs=placed,
        out_specs=(P("seq", "dp"), P("seq", "dp")),
        check_vma=False,
    )
```

```python
import contextlib
import functools
import math

import jax
import jax.numpy as jnp
from jax import lax
from jax.experimental import pallas as pl
from jax.experimental.pallas import tpu as pltpu
from jax.sharding import PartitionSpec as P

HS = 128
NEG = -1e30
LOG2E = math.log2(math.e)
MESH = pl.DeviceIdType.MESH
PARTS = 3
HOPS = 1


def mark(name):
    return contextlib.nullcontext()


def kernel(
    S, D, inv_root,
    own_s, row_s, own_h, row_h, q_h, key_h, val_h, cq_h, enc_h, w_h,
    att, crs,
    att_v, crs_v, prev_v, prev_s, q, cqr, wpart, wsend, wraw, w32, encv, wall, esel, kvs, cqs,
    acc_st, st, rin, rin_st, rout, fa, fb, named_ref,
    kall, vall, m_ref, l_ref, acc_ref,
    lsem, id_send, id_recv, id_sem,
    sz, szp, sw, rw, sws, rws, scq, scp, rcq, sra, rra, srs, rrs,
    send_k, recv_k, send_r, send_ks, recv_ks,
):
    f32, bf = jnp.float32, jnp.bfloat16
    s = lax.axis_index("seq")
    d = lax.axis_index("dp")
    k = s % 2
    g = s // 2
    c = g % 4
    base = g - c
    chips = S // 2
    sib = s + 1 - 2 * k
    nxt = (s + 1) % S
    prv = (s + S - 1) % S
    T = q.shape[0]
    near, spans_here = own_s.shape
    slots = spans_here + 1
    span_len = T // spans_here
    tile_len = encv.shape[1]
    wide = encv.shape[2]
    quarter = wide // 4
    R = cqs.shape[1]
    tail = R - T
    groups = span_len // tail
    lane_step = HS // groups
    half_step = lane_step // 2
    scale = inv_root * LOG2E

    def sq(chip):
        return {"seq": chip * 2 + k}

    bar = pltpu.get_barrier_semaphore()

    def greet(to):
        pl.semaphore_signal(bar, 1, device_id=to, device_id_type=MESH)

    greet({"seq": sib})
    greet(sq(base + (c + 1 - 2 * (c % 2))))
    greet(sq(base + (c + 2) % 4))

    @pl.when(k == 1)
    def _():
        greet({"seq": nxt})

    @pl.when(k == 0)
    def _():
        greet({"seq": prv})

    greet(sq(base + 3 - c))

    @pl.loop(1, D)
    def _(o):
        greet({"dp": (d + o) % D})

    @pl.loop(4, chips)
    def _(o):
        greet(sq((base + o) % chips))

    mine = pl.ds(2 * quarter * c, 2 * quarter)
    wfirst = pltpu.make_async_copy(w_h.at[mine], wpart, lsem.at[6])
    wfirst.start()
    wcopy = pltpu.make_async_copy(w_h, wraw, lsem.at[0])
    kcopy = pltpu.make_async_copy(key_h, kall.at[s], lsem.at[1])
    vcopy = pltpu.make_async_copy(val_h, vall.at[s], lsem.at[2])
    ccopy = pltpu.make_async_copy(cq_h, cqr, lsem.at[3])
    qcopy = pltpu.make_async_copy(q_h, q, lsem.at[4])
    ecopy = pltpu.make_async_copy(enc_h, encv, lsem.at[5])
    for cp in (wcopy, kcopy, vcopy, ccopy, qcopy, ecopy):
        cp.start()

    with mark("prep"):
        kcopy.wait()
        vcopy.wait()
        wfirst.wait()
        w32[:2 * quarter, :] = wpart[...].astype(f32)
        wsend[...] = w32[pl.ds(k, quarter, stride=2), :].astype(bf)

    def id_copy(i, ref):
        return pltpu.make_async_remote_copy(
            ref, prev_v.at[i], id_send.at[i], id_recv.at[i], device_id={"seq": nxt}, device_id_type=MESH)

    def w_copy(h, cc, to, sem):
        ref = wall.at[h, k, pl.ds(cc * quarter, quarter)]
        return pltpu.make_async_remote_copy(ref, ref, sem, rw.at[h, cc], device_id=to, device_id_type=MESH)

    xc = c + 1 - 2 * (c % 2)
    yc = (c + 2) % 4
    dc = 3 - c

    def w_plane(h):
        return [w_copy(h, c, sq(base + cc), sw.at[h, i]) for i, cc in enumerate((xc, yc, dc))]

    def w_recv(h, cc):
        w_copy(h, cc, {"seq": sib}, rw.at[h, cc]).wait_recv()

    def w_sib(h, cc, kk):
        ref = wall.at[h, kk, pl.ds(cc * quarter, quarter)]
        return pltpu.make_async_remote_copy(
            ref, ref, sws.at[h, cc], rws.at[h, cc], device_id={"seq": sib}, device_id_type=MESH)

    pair = d // 2
    pairs = D // 2
    mate = d + 1 - 2 * (d % 2)

    def entry(other, here):
        return jnp.where(other < here, 2 * here, 2 * here + 1)

    def cq_copy(h, to, sem):
        return pltpu.make_async_remote_copy(
            cqs.at[h], cqs.at[h], sem, rcq.at[h], device_id={"dp": to}, device_id_type=MESH)

    def cq_own(what):
        @pl.loop(0, pairs)
        def _(o):
            there = (pair + o) % pairs
            what(cq_copy(d, jnp.where(o == 0, mate, entry(pair, there)), scq.at[there]))

    def w_own(what):
        @pl.loop(0, pairs)
        def _(o):
            there = (pair + o) % pairs
            what(pltpu.make_async_remote_copy(
                wsend, wall.at[d, k, pl.ds(c * quarter, quarter)], sz.at[there], rw.at[d, c],
                device_id={"dp": jnp.where(o == 0, mate, entry(pair, there))}, device_id_type=MESH))

    def w_pass(h):
        return w_copy(h, c, {"dp": mate}, szp.at[h])

    def cq_pass(h):
        return cq_copy(h, mate, scp.at[h])

    def passes(h):
        return (h // 2 != pair) & (entry(h // 2, pair) == d)

    parts = ((0, kall), (1, vall))

    def kv_copy(i, land, src, to, sem):
        ref = land.at[src * 2 + k]
        return pltpu.make_async_remote_copy(
            ref, ref, sem, recv_k.at[i, src], device_id=sq(to), device_id_type=MESH)

    def kv_recv(i, land, src):
        kv_copy(i, land, src, (g + 1) % chips, recv_k.at[i, src]).wait_recv()

    def kv_sib(i, land, src, kk):
        ref = land.at[src * 2 + kk]
        return pltpu.make_async_remote_copy(
            ref, ref, send_ks.at[i, src], recv_ks.at[i, src], device_id={"seq": sib}, device_id_type=MESH)

    def kv_own(i, land, what):
        @pl.when(c == 0)
        def _():
            what(kv_copy(i, land, g, base + 1, send_k.at[i, base + 1]))
            what(kv_copy(i, land, g, base + 2, send_k.at[i, base + 2]))

        @pl.when((c == 1) | (c == 2))
        def _():
            what(kv_copy(i, land, g, base + 3, send_k.at[i, base + 3]))

        @pl.loop(base + 4, chips)
        def _(to):
            what(kv_copy(i, land, g, to, send_k.at[i, to]))

    def kv_own_sib(what):
        @pl.when(k == 0)
        def _():
            for i, land in parts:
                what(kv_sib(i, land, g, 0))

    def kv_relay(i, land, src, what):
        @pl.when((c == i + 1) & (src == base))
        def _():
            what(kv_copy(i, land, src, base + 3, send_r.at[i, src]))

        @pl.when((c == 3) & (src == base + 1))
        def _():
            what(kv_copy(i, land, src, base + 2, send_r.at[i, src]))

    dirs = (1, -1)

    def valid(h):
        return (h >= 0) & (h < D)

    with mark("barwait"):
        pl.semaphore_wait(bar, 5 + (chips - 4) + D - 1)

    w_own(lambda cp: cp.start())

    for i, ref in ((0, own_h), (1, row_h)):
        id_copy(i, ref).start()

    kv_own_sib(lambda cp: cp.start())
    kv_own(*parts[0], lambda cp: cp.start())

    step = T // 4 if T % 64 == 0 else T
    steps = [pl.ds(i, step) for i in range(0, T, step)]

    def weigh(ex, values):
        both = jnp.dot(ex.astype(bf), jnp.concatenate([values, jnp.ones_like(values)], axis=1),
                       preferred_element_type=f32)
        return both[:, :HS], both[:, HS:HS + 1]

    qcopy.wait()
    with mark("selfown"):
        for i, rows in enumerate(steps):
            seen = (i + 1) * step
            sc = lax.dot_general(q[rows, :], kall[s, :seen, :], (((1,), (1,)), ((), ())),
                                 preferred_element_type=f32) * scale
            r = lax.broadcasted_iota(jnp.int32, sc.shape, 0) + i * step
            cc = lax.broadcasted_iota(jnp.int32, sc.shape, 1)
            sc = jnp.where(cc <= r, sc, NEG)
            mx = jnp.max(sc, axis=1, keepdims=True)
            m_ref[rows, :] = mx
            acc_ref[rows, :], l_ref[rows, :] = weigh(jnp.exp2(sc - mx), vall[s, :seen, :])

    with mark("cqshift"):
        ccopy.wait()
        shifted = jnp.concatenate([cqr[...].astype(f32), jnp.zeros((tail, HS), f32)], axis=0)
        cqs[d] = pltpu.roll(shifted, 1, 0).astype(bf)
    cq_own(lambda cp: cp.start())

    with mark("wsplit"):
        wcopy.wait()
        w32[...] = wraw[...].astype(f32)
        for kv in range(2):
            wall[d, kv] = w32[pl.ds(kv, wide, stride=2), :].astype(bf)

    def attend(keys, values):
        for rows in steps:
            sc = lax.dot_general(q[rows, :], keys, (((1,), (1,)), ((), ())),
                                 preferred_element_type=f32) * scale
            old = m_ref[rows, :]
            mx = jnp.maximum(old, jnp.max(sc, axis=1, keepdims=True))
            fade = jnp.exp2(old - mx)
            m_ref[rows, :] = mx
            more, total = weigh(jnp.exp2(sc - mx), values)
            l_ref[rows, :] = l_ref[rows, :] * fade + total
            acc_ref[rows, :] = acc_ref[rows, :] * fade + more

    def find(owner_of, row_of):
        row, named = row_of(0), owner_of(0) == d
        for n in range(1, near):
            mine = owner_of(n) == d
            row = jnp.where(mine, row_of(n), row)
            named = named | mine
        return row, named

    def slot_at(j):
        if j == 0:
            return find(lambda n: prev_s[0, n, spans_here - 1], lambda n: prev_s[1, n, spans_here - 1])
        return find(lambda n: own_s[n, j - 1], lambda n: row_s[n, j - 1])

    lane = lax.broadcasted_iota(jnp.int32, (span_len, HS), 1)
    named_ref[...] = jnp.zeros_like(named_ref)

    def pick(j):
        row, named = slot_at(j)
        esel[j * tile_len:(j + 1) * tile_len, :] = encv[row]
        seen = jnp.where(named, 1.0, 0.0)
        named_ref[...] = jnp.where((lane == j) | (lane == half_step + j), seen, named_ref[...])

    per = -(-slots // PARTS)
    chunks = [range(a, min(a + per, slots)) for a in range(0, slots, per)]

    def rows_of(js):
        a = js[0] * span_len
        b = R if js[-1] == slots - 1 else (js[-1] + 1) * span_len
        return slice(a, b)

    def project(h):
        weight = jnp.concatenate([wall[h, 0], wall[h, 1]], axis=1)
        for js in chunks:
            part = pl.ds(js[0] * tile_len, len(js) * tile_len)
            kvs[h, part, :] = jnp.dot(esel[part, :], weight, preferred_element_type=f32).astype(bf)

    def cross(h):
        with mark("attn"):
            blocks = [rows_of([j]) for j in range(slots)]
            sc = jnp.concatenate(
                [lax.dot_general(cqs[h, rows, :], kvs[h, j * tile_len:(j + 1) * tile_len, :HS],
                                 (((1,), (1,)), ((), ())), preferred_element_type=f32)
                 for j, rows in enumerate(blocks)], axis=0) * scale
            mx = jnp.max(sc, axis=1, keepdims=True)
            ex = jnp.exp2(sc - mx)
            tot = []
            for j, rows in enumerate(blocks):
                values = kvs[h, j * tile_len:(j + 1) * tile_len, HS:]
                both = jnp.dot(ex[rows].astype(bf), jnp.concatenate([values, jnp.ones_like(values)], axis=1),
                               preferred_element_type=f32)
                acc_st[h, rows, :] = both[:, :HS]
                tot.append(both[:, HS:])
        with mark("pack"):
            packed = jnp.zeros((span_len, HS), f32)
            for j, rows in enumerate(blocks):
                top, sums = mx[rows], tot[j]
                n = rows.stop - rows.start
                if n < span_len:
                    top = jnp.concatenate([top, jnp.zeros((span_len - n, 1), f32)], axis=0)
                    sums = jnp.concatenate([sums, jnp.zeros((span_len - n, HS), f32)], axis=0)
                packed = jnp.where(lane == j, top, packed)
                packed = jnp.where(lane == half_step + j, sums, packed)
            packed = jnp.where(named_ref[...] > 0, packed, jnp.where(lane < half_step, NEG, 0.0))
            st[h] = sum(
                [packed[r * tail:(r + 1) * tail] if r == 0
                 else pltpu.roll(packed[r * tail:(r + 1) * tail], r * lane_step, 1) for r in range(groups)])

    def unpack(x):
        return jnp.concatenate(
            [x if r == 0 else pltpu.roll(x, HS - r * lane_step, 1) for r in range(groups)], axis=0)

    hops = [range(a, min(a + -(-slots // HOPS), slots)) for a in range(0, slots, -(-slots // HOPS))]

    def ret_copy(h, ch, slot):
        a = rows_of(hops[ch])
        part = pl.ds(a.start, a.stop - a.start)
        return pltpu.make_async_remote_copy(
            rout.at[h, part], rin.at[d, part], sra.at[h, ch], rra.at[slot, ch],
            device_id={"dp": h}, device_id_type=MESH)

    def st_copy(h, slot):
        return pltpu.make_async_remote_copy(
            st.at[h], rin_st.at[d], srs.at[h], rrs.at[slot],
            device_id={"dp": h}, device_id_type=MESH)

    packed_lane = lax.broadcasted_iota(jnp.int32, (tail, HS), 1) % lane_step

    def ship(h):
        st_copy(h, d).start()
        for ch, js in enumerate(hops):
            rows = rows_of(js)
            rout[h, rows, :] = acc_st[h, rows, :].astype(bf)
            ret_copy(h, ch, d).start()

    def merge(src):
        st_copy(mate, src).wait_recv()
        a, b = st[d], rin_st[src]
        top = jnp.maximum(a, b)
        fade_a, fade_b = jnp.exp2(a - top), jnp.exp2(b - top)
        tot = (fade_a * pltpu.roll(a, HS - half_step, 1)
               + fade_b * pltpu.roll(b, HS - half_step, 1))
        st[d] = jnp.where(packed_lane < half_step, top, pltpu.roll(tot, half_step, 1))
        fa[...] = unpack(fade_a)
        fb[...] = unpack(fade_b)
        for ch, js in enumerate(hops):
            ret_copy(mate, ch, src).wait_recv()
            for j in js:
                rows = rows_of([j])
                n = rows.stop - rows.start
                acc_st[d, rows, :] = (fa[:n, j:j + 1] * acc_st[d, rows, :]
                                      + fb[:n, j:j + 1] * rin[src, rows, :].astype(f32))

    def kv_stage(src, i, land):
        kv_recv(i, land, src)
        kv_relay(i, land, src, lambda cp: cp.start())
        kv_sib(i, land, src, k).start()

    def kv_done(src):
        for i, land in parts:
            kv_sib(i, land, src, 1 - k).wait_recv()
        attend(kall[pl.ds(src * 2, 2)].reshape(2 * T, HS), vall[pl.ds(src * 2, 2)].reshape(2 * T, HS))

    def order(i):
        return base + jnp.where(c == 3, (i + 1) % 3, i)

    def z_recv(e):
        for dirn in dirs:
            h = d - dirn * e

            @pl.when(valid(h))
            def _():
                with mark("wz"):
                    w_recv(h, c)

                    @pl.when(passes(h))
                    def _():
                        w_pass(h).start()

                    for cp in w_plane(h):
                        cp.start()
                    w_sib(h, c, k).start()

    def plane_recv(e):
        for dirn in dirs:
            h = d - dirn * e

            @pl.when(valid(h))
            def _():
                with mark("wplane"):
                    for cc in (xc, yc, dc):
                        w_recv(h, cc)
                        w_sib(h, cc, k).start()

    def cq_enter(e):
        for dirn in dirs:
            h = d - dirn * e

            @pl.when(valid(h) & passes(h))
            def _():
                with mark("cqpass"):
                    cq_pass(h).wait_recv()
                    cq_pass(h).start()

    def each_side(e, what):
        @pl.loop(0, 2)
        def _(side):
            h = d + (2 * side - 1) * e

            @pl.when(valid(h))
            def _():
                what(h)

    def prepare(h):
        with mark("wsib"):
            for cc in range(4):
                w_sib(h, cc, 1 - k).wait_recv()
        with mark("proj"):
            project(h)

    def answer(h):
        @pl.when(jnp.logical_not(passes(h)))
        def _():
            with mark("cqwait"):
                cq_pass(h).wait_recv()

        cross(h)

        ship(h)

    with mark("gather"):
        ecopy.wait()
        for j in range(1, slots):
            pick(j)

    z_recv(1)

    with mark("ids"):
        for i, ref in ((0, own_h), (1, row_h)):
            id_copy(i, ref).wait_recv()
            pltpu.make_async_copy(prev_v.at[i], prev_s.at[i], id_sem.at[i]).start()
        for i in range(2):
            pltpu.make_async_copy(prev_v.at[i], prev_s.at[i], id_sem.at[i]).wait()
        pick(0)
    with mark("projown"):
        project(d)
    pl.loop(2, D)(z_recv)
    cross(d)

    @pl.when(k == 1)
    def _():
        with mark("selfsib"):
            for i, land in parts:
                kv_sib(i, land, g, 0).wait_recv()
            attend(kall[s - 1], vall[s - 1])

    near_by = jnp.where(c > 2, 2, jnp.where(c > 0, 1, 0))

    plane_recv(1)
    cq_enter(1)

    @pl.loop(2, D + 1)
    def _(e):
        each_side(e - 1, prepare)

        @pl.when(e < D)
        def _():
            plane_recv(e)
            cq_enter(e)

        @pl.when(e == 2)
        def _():
            kv_own(*parts[1], lambda cp: cp.start())

        @pl.when(e == D - 1)
        def _():
            @pl.loop(0, near_by)
            def _(i):
                with mark("kstage"):
                    kv_stage(order(i), *parts[0])

        each_side(e - 1, answer)

    @pl.loop(0, base)
    def _(src):
        for i, land in parts:
            kv_stage(src, i, land)
        kv_done(src)

    @pl.loop(0, near_by)
    def _(i):
        with mark("vstage"):
            kv_stage(order(i), *parts[1])

    def kv_turn(i):
        @pl.when(i < near_by)
        def _():
            with mark("kvdone"):
                kv_done(order(i))

    kv_turn(0)
    kv_turn(1)

    @pl.loop(near_by, c)
    def _(i):
        with mark("laststage"):
            for j, land in parts:
                kv_stage(order(i), j, land)

    @pl.loop(near_by, c)
    def _(i):
        with mark("kvdone"):
            kv_done(order(i))

    with mark("finishatt"):
        att_v[...] = (acc_ref[...] / l_ref[...]).astype(bf)
        acopy = pltpu.make_async_copy(att_v, att, lsem.at[0])
        acopy.start()

    merge(mate)

    @pl.loop(1, pairs)
    def _(o):
        for side in (0, 1):
            with mark("mergelast"):
                there = (pair + o) % pairs
                merge(jnp.where((there < pair) == (side == 0), 2 * there + 1, 2 * there))

    with mark("finish"):
        tots = unpack(pltpu.roll(st[d], HS - half_step, 1))
        for j in range(slots):
            rows = rows_of([j])
            n = rows.stop - rows.start
            out = acc_st[d, rows, :] / tots[:n, j:j + 1]
            if j == 0:
                out = jnp.where(s > 0, out, 0.0)
            acc_st[d, rows, :] = out
        crs_v[...] = pltpu.roll(acc_st[d], R - 1, 0)[:T].astype(bf)
        ccopy = pltpu.make_async_copy(crs_v, crs, lsem.at[1])
        ccopy.start()

    with mark("drain"):
        for i, ref in ((0, own_h), (1, row_h)):
            id_copy(i, ref).wait_send()

        w_own(lambda cp: cp.wait_send())
        cq_own(lambda cp: cp.wait_send())

        @pl.loop(1, D)
        def _(o):
            h = (d + o) % D

            @pl.when(passes(h))
            def _():
                cq_pass(h).wait_send()
                w_pass(h).wait_send()

            for cp in w_plane(h):
                cp.wait_send()
            for cc in range(4):
                w_sib(h, cc, k).wait_send()
            st_copy(h, d).wait_send()
            for ch in range(len(hops)):
                ret_copy(h, ch, d).wait_send()

        for i, land in parts:
            kv_own(i, land, lambda cp: cp.wait_send())
        kv_own_sib(lambda cp: cp.wait_send())

        @pl.loop(0, g)
        def _(src):
            for i, land in parts:
                kv_relay(i, land, src, lambda cp: cp.wait_send())
                kv_sib(i, land, src, k).wait_send()

        acopy.wait()
        ccopy.wait()


def on_device(queries, keys, values, cross_queries, encoded, cross_kv_weight, owners, tile_rows):
    S, D = lax.axis_size("seq"), lax.axis_size("dp")
    T, width = queries.shape
    pool_here, tile_len, wide = encoded.shape
    spans_here = owners.shape[0]
    slots = spans_here + 1
    span_len = T // spans_here
    R = T + 16
    w = cross_kv_weight.reshape(2 * wide, HS)
    own, row = owners.T, tile_rows.T
    near = own.shape[0]
    chips = S // 2
    bf, f32 = jnp.bfloat16, jnp.float32
    hbm = pl.BlockSpec(memory_space=pl.ANY)
    dma = pltpu.SemaphoreType.DMA
    attended, crossed = pl.pallas_call(
        functools.partial(kernel, S, D, 1.0 / math.sqrt(HS)),
        name="retro",
        out_shape=(jax.ShapeDtypeStruct((T, width), bf), jax.ShapeDtypeStruct((T, width), bf)),
        in_specs=[pl.BlockSpec(memory_space=pltpu.SMEM)] * 2 + [hbm] * 8,
        out_specs=(hbm, hbm),
        scratch_shapes=[
            pltpu.VMEM((T, HS), bf),
            pltpu.VMEM((T, HS), bf),
            pltpu.VMEM((2, near, spans_here), jnp.int32),
            pltpu.SMEM((2, near, spans_here), jnp.int32),
            pltpu.VMEM((T, HS), bf),
            pltpu.VMEM((T, HS), bf),
            pltpu.VMEM((wide // 2, HS), bf),
            pltpu.VMEM((wide // 4, HS), bf),
            pltpu.VMEM((2 * wide, HS), bf),
            pltpu.VMEM((2 * wide, HS), f32),
            pltpu.VMEM((pool_here, tile_len, wide), bf),
            pltpu.VMEM((D, 2, wide, HS), bf),
            pltpu.VMEM((slots * tile_len, wide), bf),
            pltpu.VMEM((D, slots * tile_len, 2 * HS), bf),
            pltpu.VMEM((D, R, HS), bf),
            pltpu.VMEM((D, R, HS), f32),
            pltpu.VMEM((D, 16, HS), f32),
            pltpu.VMEM((D, R, HS), bf),
            pltpu.VMEM((D, 16, HS), f32),
            pltpu.VMEM((D, R, HS), bf),
            pltpu.VMEM((span_len, HS), f32),
            pltpu.VMEM((span_len, HS), f32),
            pltpu.VMEM((span_len, HS), f32),
            pltpu.VMEM((S, T, HS), bf),
            pltpu.VMEM((S, T, HS), bf),
            pltpu.VMEM((T, 1), f32),
            pltpu.VMEM((T, 1), f32),
            pltpu.VMEM((T, HS), f32),
            dma((7,)), dma((2,)), dma((2,)), dma((2,)),
            dma((D // 2,)), dma((D,)), dma((D, 3)), dma((D, 4)), dma((D, 4)), dma((D, 4)), dma((D // 2,)), dma((D,)), dma((D,)),
            dma((D, HOPS)), dma((D, HOPS)), dma((D,)), dma((D,)),
            dma((2, chips)), dma((2, chips)), dma((2, chips)), dma((2, chips)), dma((2, chips)),
        ],
        compiler_params=pltpu.CompilerParams(
            collective_id=0, has_side_effects=True, vmem_limit_bytes=60 * 1024 * 1024),
    )(own, row, own, row, queries, keys, values, cross_queries, encoded, w)
    return attended, crossed


def solution(mesh):
    placed = (
        P("seq", "dp"),
        P("seq", "dp"),
        P("seq", "dp"),
        P("seq", "dp"),
        P("dp", None, None),
        P(None, None, "dp"),
        P("seq", None),
        P("seq", None),
    )
    return jax.shard_map(
        on_device,
        mesh=mesh,
        in_specs=placed,
        out_specs=(P("seq", "dp"), P("seq", "dp")),
        check_vma=False,
    )
```

```python
import contextlib
import functools
import math

import jax
import jax.numpy as jnp
from jax import lax
from jax.experimental import pallas as pl
from jax.experimental.pallas import tpu as pltpu
from jax.sharding import PartitionSpec as P

HS = 128
NEG = -1e30
LOG2E = math.log2(math.e)
MESH = pl.DeviceIdType.MESH
PARTS = 3
HOPS = 1


def mark(name):
    return contextlib.nullcontext()


def kernel(
    S, D, inv_root,
    own_s, row_s, own_h, row_h, q_h, key_h, val_h, cq_h, enc_h, w_h,
    both_h,
    att_v, crs_v, prev_v, prev_s, q, cqr, wpart, wsend, wraw, w32, encv, wall, esel, kvs, cqs,
    acc_st, st, rin, rin_st, rout, fa, fb, named_ref,
    kall, vall, m_ref, l_ref, acc_ref,
    lsem, id_send, id_recv, id_sem,
    sz, szp, sw, rw, sws, rws, scq, scp, rcq, sra, rra, srs, rrs,
    send_k, recv_k, send_r, send_ks, recv_ks,
):
    f32, bf = jnp.float32, jnp.bfloat16
    s = lax.axis_index("seq")
    d = lax.axis_index("dp")
    k = s % 2
    g = s // 2
    c = g % 4
    base = g - c
    chips = S // 2
    sib = s + 1 - 2 * k
    nxt = (s + 1) % S
    prv = (s + S - 1) % S
    T = q.shape[0]
    near, spans_here = own_s.shape
    slots = spans_here + 1
    span_len = T // spans_here
    tile_len = encv.shape[1]
    wide = encv.shape[2]
    quarter = wide // 4
    R = cqs.shape[1]
    tail = R - T
    groups = span_len // tail
    lane_step = HS // groups
    half_step = lane_step // 2
    scale = inv_root * LOG2E

    def sq(chip):
        return {"seq": chip * 2 + k}

    bar = pltpu.get_barrier_semaphore()

    def greet(to):
        pl.semaphore_signal(bar, 1, device_id=to, device_id_type=MESH)

    greet({"seq": sib})
    greet(sq(base + (c + 1 - 2 * (c % 2))))
    greet(sq(base + (c + 2) % 4))

    @pl.when(k == 1)
    def _():
        greet({"seq": nxt})

    @pl.when(k == 0)
    def _():
        greet({"seq": prv})

    greet(sq(base + 3 - c))

    @pl.loop(1, D)
    def _(o):
        greet({"dp": (d + o) % D})

    @pl.loop(4, chips)
    def _(o):
        greet(sq((base + o) % chips))

    mine = pl.ds(2 * quarter * c, 2 * quarter)
    wfirst = pltpu.make_async_copy(w_h.at[mine], wpart, lsem.at[6])
    wfirst.start()
    wcopy = pltpu.make_async_copy(w_h, wraw, lsem.at[0])
    kcopy = pltpu.make_async_copy(key_h, kall.at[s], lsem.at[1])
    vcopy = pltpu.make_async_copy(val_h, vall.at[s], lsem.at[2])
    ccopy = pltpu.make_async_copy(cq_h, cqr, lsem.at[3])
    qcopy = pltpu.make_async_copy(q_h, q, lsem.at[4])
    ecopy = pltpu.make_async_copy(enc_h, encv, lsem.at[5])
    for cp in (wcopy, kcopy, vcopy, ccopy, qcopy, ecopy):
        cp.start()

    with mark("prep"):
        kcopy.wait()
        vcopy.wait()
        wfirst.wait()
        w32[:2 * quarter, :] = wpart[...].astype(f32)
        wsend[...] = w32[pl.ds(k, quarter, stride=2), :].astype(bf)

    def id_copy(i, ref):
        return pltpu.make_async_remote_copy(
            ref, prev_v.at[i], id_send.at[i], id_recv.at[i], device_id={"seq": nxt}, device_id_type=MESH)

    def w_copy(h, cc, to, sem):
        ref = wall.at[h, k, pl.ds(cc * quarter, quarter)]
        return pltpu.make_async_remote_copy(ref, ref, sem, rw.at[h, cc], device_id=to, device_id_type=MESH)

    xc = c + 1 - 2 * (c % 2)
    yc = (c + 2) % 4
    dc = 3 - c

    def w_plane(h):
        return [w_copy(h, c, sq(base + cc), sw.at[h, i]) for i, cc in enumerate((xc, yc, dc))]

    def w_recv(h, cc):
        w_copy(h, cc, {"seq": sib}, rw.at[h, cc]).wait_recv()

    def w_sib(h, cc, kk):
        ref = wall.at[h, kk, pl.ds(cc * quarter, quarter)]
        return pltpu.make_async_remote_copy(
            ref, ref, sws.at[h, cc], rws.at[h, cc], device_id={"seq": sib}, device_id_type=MESH)

    pair = d // 2
    pairs = D // 2
    mate = d + 1 - 2 * (d % 2)

    def entry(other, here):
        return jnp.where(other < here, 2 * here, 2 * here + 1)

    def cq_copy(h, to, sem):
        return pltpu.make_async_remote_copy(
            cqs.at[h], cqs.at[h], sem, rcq.at[h], device_id={"dp": to}, device_id_type=MESH)

    def cq_own(what):
        @pl.loop(0, pairs)
        def _(o):
            there = (pair + o) % pairs
            what(cq_copy(d, jnp.where(o == 0, mate, entry(pair, there)), scq.at[there]))

    def w_own(what):
        @pl.loop(0, pairs)
        def _(o):
            there = (pair + o) % pairs
            what(pltpu.make_async_remote_copy(
                wsend, wall.at[d, k, pl.ds(c * quarter, quarter)], sz.at[there], rw.at[d, c],
                device_id={"dp": jnp.where(o == 0, mate, entry(pair, there))}, device_id_type=MESH))

    def w_pass(h):
        return w_copy(h, c, {"dp": mate}, szp.at[h])

    def cq_pass(h):
        return cq_copy(h, mate, scp.at[h])

    def passes(h):
        return (h // 2 != pair) & (entry(h // 2, pair) == d)

    parts = ((0, kall), (1, vall))

    def kv_copy(i, land, src, to, sem):
        ref = land.at[src * 2 + k]
        return pltpu.make_async_remote_copy(
            ref, ref, sem, recv_k.at[i, src], device_id=sq(to), device_id_type=MESH)

    def kv_recv(i, land, src):
        kv_copy(i, land, src, (g + 1) % chips, recv_k.at[i, src]).wait_recv()

    def kv_sib(i, land, src, kk):
        ref = land.at[src * 2 + kk]
        return pltpu.make_async_remote_copy(
            ref, ref, send_ks.at[i, src], recv_ks.at[i, src], device_id={"seq": sib}, device_id_type=MESH)

    def kv_own(i, land, what):
        @pl.when(c == 0)
        def _():
            what(kv_copy(i, land, g, base + 1, send_k.at[i, base + 1]))
            what(kv_copy(i, land, g, base + 2, send_k.at[i, base + 2]))

        @pl.when((c == 1) | (c == 2))
        def _():
            what(kv_copy(i, land, g, base + 3, send_k.at[i, base + 3]))

        @pl.loop(base + 4, chips)
        def _(to):
            what(kv_copy(i, land, g, to, send_k.at[i, to]))

    def kv_own_sib(what):
        @pl.when(k == 0)
        def _():
            for i, land in parts:
                what(kv_sib(i, land, g, 0))

    def kv_relay(i, land, src, what):
        @pl.when((c == i + 1) & (src == base))
        def _():
            what(kv_copy(i, land, src, base + 3, send_r.at[i, src]))

        @pl.when((c == 3) & (src == base + 1))
        def _():
            what(kv_copy(i, land, src, base + 2, send_r.at[i, src]))

    dirs = (1, -1)

    def valid(h):
        return (h >= 0) & (h < D)

    with mark("barwait"):
        pl.semaphore_wait(bar, 5 + (chips - 4) + D - 1)

    w_own(lambda cp: cp.start())

    for i, ref in ((0, own_h), (1, row_h)):
        id_copy(i, ref).start()

    kv_own_sib(lambda cp: cp.start())

    step = T // 4 if T % 64 == 0 else T
    steps = [pl.ds(i, step) for i in range(0, T, step)]

    def weigh(ex, values):
        both = jnp.dot(ex.astype(bf), jnp.concatenate([values, jnp.ones_like(values)], axis=1),
                       preferred_element_type=f32)
        return both[:, :HS], both[:, HS:HS + 1]

    qcopy.wait()
    with mark("selfown"):
        for i, rows in enumerate(steps):
            seen = (i + 1) * step
            sc = lax.dot_general(q[rows, :], kall[s, :seen, :], (((1,), (1,)), ((), ())),
                                 preferred_element_type=f32) * scale
            r = lax.broadcasted_iota(jnp.int32, sc.shape, 0) + i * step
            cc = lax.broadcasted_iota(jnp.int32, sc.shape, 1)
            sc = jnp.where(cc <= r, sc, NEG)
            mx = jnp.max(sc, axis=1, keepdims=True)
            m_ref[rows, :] = mx
            acc_ref[rows, :], l_ref[rows, :] = weigh(jnp.exp2(sc - mx), vall[s, :seen, :])

    with mark("cqshift"):
        ccopy.wait()
        shifted = jnp.concatenate([cqr[...].astype(f32), jnp.zeros((tail, HS), f32)], axis=0)
        cqs[d] = pltpu.roll(shifted, 1, 0).astype(bf)
    cq_own(lambda cp: cp.start())

    with mark("wsplit"):
        wcopy.wait()
        w32[...] = wraw[...].astype(f32)
        for kv in range(2):
            wall[d, kv] = w32[pl.ds(kv, wide, stride=2), :].astype(bf)

    def attend(keys, values):
        for rows in steps:
            sc = lax.dot_general(q[rows, :], keys, (((1,), (1,)), ((), ())),
                                 preferred_element_type=f32) * scale
            old = m_ref[rows, :]
            mx = jnp.maximum(old, jnp.max(sc, axis=1, keepdims=True))
            fade = jnp.exp2(old - mx)
            m_ref[rows, :] = mx
            more, total = weigh(jnp.exp2(sc - mx), values)
            l_ref[rows, :] = l_ref[rows, :] * fade + total
            acc_ref[rows, :] = acc_ref[rows, :] * fade + more

    def find(owner_of, row_of):
        row, named = row_of(0), owner_of(0) == d
        for n in range(1, near):
            mine = owner_of(n) == d
            row = jnp.where(mine, row_of(n), row)
            named = named | mine
        return row, named

    def slot_at(j):
        if j == 0:
            return find(lambda n: prev_s[0, n, spans_here - 1], lambda n: prev_s[1, n, spans_here - 1])
        return find(lambda n: own_s[n, j - 1], lambda n: row_s[n, j - 1])

    lane = lax.broadcasted_iota(jnp.int32, (span_len, HS), 1)
    named_ref[...] = jnp.zeros_like(named_ref)

    def pick(j):
        row, named = slot_at(j)
        esel[j * tile_len:(j + 1) * tile_len, :] = encv[row]
        seen = jnp.where(named, 1.0, 0.0)
        named_ref[...] = jnp.where((lane == j) | (lane == half_step + j), seen, named_ref[...])

    per = -(-slots // PARTS)
    chunks = [range(a, min(a + per, slots)) for a in range(0, slots, per)]

    def rows_of(js):
        a = js[0] * span_len
        b = R if js[-1] == slots - 1 else (js[-1] + 1) * span_len
        return slice(a, b)

    def project(h):
        weight = jnp.concatenate([wall[h, 0], wall[h, 1]], axis=1)
        for js in chunks:
            part = pl.ds(js[0] * tile_len, len(js) * tile_len)
            kvs[h, part, :] = jnp.dot(esel[part, :], weight, preferred_element_type=f32).astype(bf)

    def cross(h):
        with mark("attn"):
            blocks = [rows_of([j]) for j in range(slots)]
            sc = jnp.concatenate(
                [lax.dot_general(cqs[h, rows, :], kvs[h, j * tile_len:(j + 1) * tile_len, :HS],
                                 (((1,), (1,)), ((), ())), preferred_element_type=f32)
                 for j, rows in enumerate(blocks)], axis=0) * scale
            mx = jnp.max(sc, axis=1, keepdims=True)
            ex = jnp.exp2(sc - mx)
            tot = []
            for j, rows in enumerate(blocks):
                values = kvs[h, j * tile_len:(j + 1) * tile_len, HS:]
                both = jnp.dot(ex[rows].astype(bf), jnp.concatenate([values, jnp.ones_like(values)], axis=1),
                               preferred_element_type=f32)
                acc_st[h, rows, :] = both[:, :HS]
                tot.append(both[:, HS:])
        with mark("pack"):
            packed = jnp.zeros((span_len, HS), f32)
            for j, rows in enumerate(blocks):
                top, sums = mx[rows], tot[j]
                n = rows.stop - rows.start
                if n < span_len:
                    top = jnp.concatenate([top, jnp.zeros((span_len - n, 1), f32)], axis=0)
                    sums = jnp.concatenate([sums, jnp.zeros((span_len - n, HS), f32)], axis=0)
                packed = jnp.where(lane == j, top, packed)
                packed = jnp.where(lane == half_step + j, sums, packed)
            packed = jnp.where(named_ref[...] > 0, packed, jnp.where(lane < half_step, NEG, 0.0))
            st[h] = sum(
                [packed[r * tail:(r + 1) * tail] if r == 0
                 else pltpu.roll(packed[r * tail:(r + 1) * tail], r * lane_step, 1) for r in range(groups)])

    def unpack(x):
        return jnp.concatenate(
            [x if r == 0 else pltpu.roll(x, HS - r * lane_step, 1) for r in range(groups)], axis=0)

    hops = [range(a, min(a + -(-slots // HOPS), slots)) for a in range(0, slots, -(-slots // HOPS))]

    def ret_copy(h, ch, slot):
        a = rows_of(hops[ch])
        part = pl.ds(a.start, a.stop - a.start)
        return pltpu.make_async_remote_copy(
            rout.at[h, part], rin.at[d, part], sra.at[h, ch], rra.at[slot, ch],
            device_id={"dp": h}, device_id_type=MESH)

    def st_copy(h, slot):
        return pltpu.make_async_remote_copy(
            st.at[h], rin_st.at[d], srs.at[h], rrs.at[slot],
            device_id={"dp": h}, device_id_type=MESH)

    packed_lane = lax.broadcasted_iota(jnp.int32, (tail, HS), 1) % lane_step

    def ship(h):
        st_copy(h, d).start()
        for ch, js in enumerate(hops):
            rows = rows_of(js)
            rout[h, rows, :] = acc_st[h, rows, :].astype(bf)
            ret_copy(h, ch, d).start()

    def merge(src):
        st_copy(mate, src).wait_recv()
        a, b = st[d], rin_st[src]
        top = jnp.maximum(a, b)
        fade_a, fade_b = jnp.exp2(a - top), jnp.exp2(b - top)
        tot = (fade_a * pltpu.roll(a, HS - half_step, 1)
               + fade_b * pltpu.roll(b, HS - half_step, 1))
        st[d] = jnp.where(packed_lane < half_step, top, pltpu.roll(tot, half_step, 1))
        fa[...] = unpack(fade_a)
        fb[...] = unpack(fade_b)
        for ch, js in enumerate(hops):
            ret_copy(mate, ch, src).wait_recv()
            for j in js:
                rows = rows_of([j])
                n = rows.stop - rows.start
                acc_st[d, rows, :] = (fa[:n, j:j + 1] * acc_st[d, rows, :]
                                      + fb[:n, j:j + 1] * rin[src, rows, :].astype(f32))

    def kv_stage(src, i, land):
        kv_recv(i, land, src)
        kv_relay(i, land, src, lambda cp: cp.start())
        kv_sib(i, land, src, k).start()

    def kv_done(src):
        for i, land in parts:
            kv_sib(i, land, src, 1 - k).wait_recv()
        attend(kall[pl.ds(src * 2, 2)].reshape(2 * T, HS), vall[pl.ds(src * 2, 2)].reshape(2 * T, HS))

    def order(i):
        return base + jnp.where(c == 3, (i + 1) % 3, i)

    def z_recv(e):
        for dirn in dirs:
            h = d - dirn * e

            @pl.when(valid(h))
            def _():
                with mark("wz"):
                    w_recv(h, c)

                    @pl.when(passes(h))
                    def _():
                        w_pass(h).start()

                    for cp in w_plane(h):
                        cp.start()
                    w_sib(h, c, k).start()

    def plane_recv(e):
        for dirn in dirs:
            h = d - dirn * e

            @pl.when(valid(h))
            def _():
                with mark("wplane"):
                    for cc in (xc, yc, dc):
                        w_recv(h, cc)
                        w_sib(h, cc, k).start()

    def cq_enter(e):
        for dirn in dirs:
            h = d - dirn * e

            @pl.when(valid(h) & passes(h))
            def _():
                with mark("cqpass"):
                    cq_pass(h).wait_recv()
                    cq_pass(h).start()

    def each_side(e, what):
        @pl.loop(0, 2)
        def _(side):
            h = d + (2 * side - 1) * e

            @pl.when(valid(h))
            def _():
                what(h)

    def prepare(h):
        with mark("wsib"):
            for cc in range(4):
                w_sib(h, cc, 1 - k).wait_recv()
        with mark("proj"):
            project(h)

    def answer(h):
        @pl.when(jnp.logical_not(passes(h)))
        def _():
            with mark("cqwait"):
                cq_pass(h).wait_recv()

        cross(h)

        ship(h)

    with mark("gather"):
        ecopy.wait()
        for j in range(1, slots):
            pick(j)

    z_recv(1)

    with mark("ids"):
        for i, ref in ((0, own_h), (1, row_h)):
            id_copy(i, ref).wait_recv()
            pltpu.make_async_copy(prev_v.at[i], prev_s.at[i], id_sem.at[i]).start()
        for i in range(2):
            pltpu.make_async_copy(prev_v.at[i], prev_s.at[i], id_sem.at[i]).wait()
        pick(0)
    with mark("projown"):
        project(d)
    pl.loop(2, D)(z_recv)
    cross(d)

    @pl.when(k == 1)
    def _():
        with mark("selfsib"):
            for i, land in parts:
                kv_sib(i, land, g, 0).wait_recv()
            attend(kall[s - 1], vall[s - 1])

    near_by = jnp.where(c > 2, 2, jnp.where(c > 0, 1, 0))

    cq_enter(1)
    plane_recv(1)
    for i, land in parts:
        kv_own(i, land, lambda cp: cp.start())

    @pl.loop(2, D + 1)
    def _(e):
        each_side(e - 1, prepare)

        @pl.when(e < D)
        def _():
            plane_recv(e)
            cq_enter(e)

        each_side(e - 1, answer)

    @pl.loop(0, base)
    def _(src):
        for i, land in parts:
            kv_stage(src, i, land)
        kv_done(src)

    @pl.loop(0, near_by)
    def _(i):
        with mark("kstage"):
            kv_stage(order(i), *parts[0])

    @pl.loop(0, near_by)
    def _(i):
        with mark("vstage"):
            kv_stage(order(i), *parts[1])

    def kv_turn(i):
        @pl.when(i < near_by)
        def _():
            with mark("kvdone"):
                kv_done(order(i))

    kv_turn(0)
    kv_turn(1)

    @pl.loop(near_by, c)
    def _(i):
        with mark("laststage"):
            for j, land in parts:
                kv_stage(order(i), j, land)

    @pl.loop(near_by, c)
    def _(i):
        with mark("kvdone"):
            kv_done(order(i))

    with mark("finishatt"):
        att_v[...] = (acc_ref[...] / l_ref[...]).astype(bf)
        acopy = pltpu.make_async_copy(att_v, both_h.at[0], lsem.at[0])
        acopy.start()

    merge(mate)

    @pl.loop(1, pairs)
    def _(o):
        for side in (0, 1):
            with mark("mergelast"):
                there = (pair + o) % pairs
                merge(jnp.where((there < pair) == (side == 0), 2 * there + 1, 2 * there))

    with mark("finish"):
        tots = unpack(pltpu.roll(st[d], HS - half_step, 1))
        for j in range(slots):
            rows = rows_of([j])
            n = rows.stop - rows.start
            out = acc_st[d, rows, :] / tots[:n, j:j + 1]
            if j == 0:
                out = jnp.where(s > 0, out, 0.0)
            acc_st[d, rows, :] = out
        crs_v[...] = pltpu.roll(acc_st[d], R - 1, 0)[:T].astype(bf)
        ccopy = pltpu.make_async_copy(crs_v, both_h.at[1], lsem.at[1])
        ccopy.start()

    with mark("drain"):
        for i, ref in ((0, own_h), (1, row_h)):
            id_copy(i, ref).wait_send()

        w_own(lambda cp: cp.wait_send())
        cq_own(lambda cp: cp.wait_send())

        @pl.loop(1, D)
        def _(o):
            h = (d + o) % D

            @pl.when(passes(h))
            def _():
                cq_pass(h).wait_send()
                w_pass(h).wait_send()

            for cp in w_plane(h):
                cp.wait_send()
            for cc in range(4):
                w_sib(h, cc, k).wait_send()
            st_copy(h, d).wait_send()
            for ch in range(len(hops)):
                ret_copy(h, ch, d).wait_send()

        for i, land in parts:
            kv_own(i, land, lambda cp: cp.wait_send())
        kv_own_sib(lambda cp: cp.wait_send())

        @pl.loop(0, g)
        def _(src):
            for i, land in parts:
                kv_relay(i, land, src, lambda cp: cp.wait_send())
                kv_sib(i, land, src, k).wait_send()

        acopy.wait()
        ccopy.wait()


def on_device(queries, keys, values, cross_queries, encoded, cross_kv_weight, owners, tile_rows):
    S, D = lax.axis_size("seq"), lax.axis_size("dp")
    T, width = queries.shape
    pool_here, tile_len, wide = encoded.shape
    spans_here = owners.shape[0]
    slots = spans_here + 1
    span_len = T // spans_here
    R = T + 16
    w = cross_kv_weight.reshape(2 * wide, HS)
    own, row = owners.T, tile_rows.T
    near = own.shape[0]
    chips = S // 2
    bf, f32 = jnp.bfloat16, jnp.float32
    hbm = pl.BlockSpec(memory_space=pl.ANY)
    dma = pltpu.SemaphoreType.DMA
    both = pl.pallas_call(
        functools.partial(kernel, S, D, 1.0 / math.sqrt(HS)),
        name="retro",
        out_shape=jax.ShapeDtypeStruct((2, T, width), bf),
        in_specs=[pl.BlockSpec(memory_space=pltpu.SMEM)] * 2 + [hbm] * 8,
        out_specs=hbm,
        scratch_shapes=[
            pltpu.VMEM((T, HS), bf),
            pltpu.VMEM((T, HS), bf),
            pltpu.VMEM((2, near, spans_here), jnp.int32),
            pltpu.SMEM((2, near, spans_here), jnp.int32),
            pltpu.VMEM((T, HS), bf),
            pltpu.VMEM((T, HS), bf),
            pltpu.VMEM((wide // 2, HS), bf),
            pltpu.VMEM((wide // 4, HS), bf),
            pltpu.VMEM((2 * wide, HS), bf),
            pltpu.VMEM((2 * wide, HS), f32),
            pltpu.VMEM((pool_here, tile_len, wide), bf),
            pltpu.VMEM((D, 2, wide, HS), bf),
            pltpu.VMEM((slots * tile_len, wide), bf),
            pltpu.VMEM((D, slots * tile_len, 2 * HS), bf),
            pltpu.VMEM((D, R, HS), bf),
            pltpu.VMEM((D, R, HS), f32),
            pltpu.VMEM((D, 16, HS), f32),
            pltpu.VMEM((D, R, HS), bf),
            pltpu.VMEM((D, 16, HS), f32),
            pltpu.VMEM((D, R, HS), bf),
            pltpu.VMEM((span_len, HS), f32),
            pltpu.VMEM((span_len, HS), f32),
            pltpu.VMEM((span_len, HS), f32),
            pltpu.VMEM((S, T, HS), bf),
            pltpu.VMEM((S, T, HS), bf),
            pltpu.VMEM((T, 1), f32),
            pltpu.VMEM((T, 1), f32),
            pltpu.VMEM((T, HS), f32),
            dma((7,)), dma((2,)), dma((2,)), dma((2,)),
            dma((D // 2,)), dma((D,)), dma((D, 3)), dma((D, 4)), dma((D, 4)), dma((D, 4)), dma((D // 2,)), dma((D,)), dma((D,)),
            dma((D, HOPS)), dma((D, HOPS)), dma((D,)), dma((D,)),
            dma((2, chips)), dma((2, chips)), dma((2, chips)), dma((2, chips)), dma((2, chips)),
        ],
        compiler_params=pltpu.CompilerParams(
            collective_id=0, has_side_effects=True, vmem_limit_bytes=60 * 1024 * 1024),
    )(own, row, own, row, queries, keys, values, cross_queries, encoded, w)
    return both[0], both[1]


def solution(mesh):
    placed = (
        P("seq", "dp"),
        P("seq", "dp"),
        P("seq", "dp"),
        P("seq", "dp"),
        P("dp", None, None),
        P(None, None, "dp"),
        P("seq", None),
        P("seq", None),
    )
    return jax.shard_map(
        on_device,
        mesh=mesh,
        in_specs=placed,
        out_specs=(P("seq", "dp"), P("seq", "dp")),
        check_vma=False,
    )
```

```python
import contextlib
import functools
import math

import jax
import jax.numpy as jnp
from jax import lax
from jax.experimental import pallas as pl
from jax.experimental.pallas import tpu as pltpu
from jax.sharding import PartitionSpec as P

HS = 128
NEG = -1e30
LOG2E = math.log2(math.e)
MESH = pl.DeviceIdType.MESH
PARTS = 3
HOPS = 1


def mark(name):
    return contextlib.nullcontext()


def kernel(
    S, D, inv_root,
    own_s, row_s, own_h, row_h, q_h, key_h, val_h, cq_h, enc_h, w_h,
    both_h,
    att_v, crs_v, prev_v, prev_s, q, cqr, wpart, wsend, wraw, w32, encv, wall, esel, kvs, cqs,
    acc_st, st, rin, rin_st, rout, fa, fb, named_ref,
    kall, vall, m_ref, l_ref, acc_ref,
    lsem, id_send, id_recv, id_sem,
    sz, szp, sw, rw, sws, rws, scq, scp, rcq, sra, rra, srs, rrs,
    send_k, recv_k, send_r, send_ks, recv_ks,
):
    f32, bf = jnp.float32, jnp.bfloat16
    s = lax.axis_index("seq")
    d = lax.axis_index("dp")
    k = s % 2
    g = s // 2
    c = g % 4
    base = g - c
    chips = S // 2
    sib = s + 1 - 2 * k
    nxt = (s + 1) % S
    prv = (s + S - 1) % S
    T = q.shape[0]
    near, spans_here = own_s.shape
    slots = spans_here + 1
    span_len = T // spans_here
    tile_len = encv.shape[1]
    wide = encv.shape[2]
    quarter = wide // 4
    R = cqs.shape[1]
    tail = R - T
    groups = span_len // tail
    lane_step = HS // groups
    half_step = lane_step // 2
    scale = inv_root * LOG2E

    def sq(chip):
        return {"seq": chip * 2 + k}

    mine = pl.ds(2 * quarter * c, 2 * quarter)
    wfirst = pltpu.make_async_copy(w_h.at[mine], wpart, lsem.at[6])
    wfirst.start()
    wcopy = pltpu.make_async_copy(w_h, wraw, lsem.at[0])
    kcopy = pltpu.make_async_copy(key_h, kall.at[s], lsem.at[1])
    vcopy = pltpu.make_async_copy(val_h, vall.at[s], lsem.at[2])
    ccopy = pltpu.make_async_copy(cq_h, cqr, lsem.at[3])
    qcopy = pltpu.make_async_copy(q_h, q, lsem.at[4])
    ecopy = pltpu.make_async_copy(enc_h, encv, lsem.at[5])
    for cp in (kcopy, vcopy, qcopy):
        cp.start()

    bar = pltpu.get_barrier_semaphore()

    def greet(to):
        pl.semaphore_signal(bar, 1, device_id=to, device_id_type=MESH)

    greet({"seq": sib})
    greet(sq(base + (c + 1 - 2 * (c % 2))))
    greet(sq(base + (c + 2) % 4))

    @pl.when(k == 1)
    def _():
        greet({"seq": nxt})

    @pl.when(k == 0)
    def _():
        greet({"seq": prv})

    greet(sq(base + 3 - c))

    @pl.loop(1, D)
    def _(o):
        greet({"dp": (d + o) % D})

    @pl.loop(4, chips)
    def _(o):
        greet(sq((base + o) % chips))

    for cp in (ccopy, wcopy, ecopy):
        cp.start()

    with mark("prep"):
        kcopy.wait()
        vcopy.wait()
        wfirst.wait()
        w32[:2 * quarter, :] = wpart[...].astype(f32)
        wsend[...] = w32[pl.ds(k, quarter, stride=2), :].astype(bf)

    def id_copy(i, ref):
        return pltpu.make_async_remote_copy(
            ref, prev_v.at[i], id_send.at[i], id_recv.at[i], device_id={"seq": nxt}, device_id_type=MESH)

    def w_copy(h, cc, to, sem):
        ref = wall.at[h, k, pl.ds(cc * quarter, quarter)]
        return pltpu.make_async_remote_copy(ref, ref, sem, rw.at[h, cc], device_id=to, device_id_type=MESH)

    xc = c + 1 - 2 * (c % 2)
    yc = (c + 2) % 4
    dc = 3 - c

    def w_plane(h):
        return [w_copy(h, c, sq(base + cc), sw.at[h, i]) for i, cc in enumerate((xc, yc, dc))]

    def w_recv(h, cc):
        w_copy(h, cc, {"seq": sib}, rw.at[h, cc]).wait_recv()

    def w_sib(h, cc, kk):
        ref = wall.at[h, kk, pl.ds(cc * quarter, quarter)]
        return pltpu.make_async_remote_copy(
            ref, ref, sws.at[h, cc], rws.at[h, cc], device_id={"seq": sib}, device_id_type=MESH)

    pair = d // 2
    pairs = D // 2
    mate = d + 1 - 2 * (d % 2)

    def entry(other, here):
        return jnp.where(other < here, 2 * here, 2 * here + 1)

    def cq_copy(h, to, sem):
        return pltpu.make_async_remote_copy(
            cqs.at[h], cqs.at[h], sem, rcq.at[h], device_id={"dp": to}, device_id_type=MESH)

    def cq_own(what):
        @pl.loop(0, pairs)
        def _(o):
            there = (pair + o) % pairs
            what(cq_copy(d, jnp.where(o == 0, mate, entry(pair, there)), scq.at[there]))

    def w_own(what):
        @pl.loop(0, pairs)
        def _(o):
            there = (pair + o) % pairs
            what(pltpu.make_async_remote_copy(
                wsend, wall.at[d, k, pl.ds(c * quarter, quarter)], sz.at[there], rw.at[d, c],
                device_id={"dp": jnp.where(o == 0, mate, entry(pair, there))}, device_id_type=MESH))

    def w_pass(h):
        return w_copy(h, c, {"dp": mate}, szp.at[h])

    def cq_pass(h):
        return cq_copy(h, mate, scp.at[h])

    def passes(h):
        return (h // 2 != pair) & (entry(h // 2, pair) == d)

    parts = ((0, kall), (1, vall))

    def kv_copy(i, land, src, to, sem):
        ref = land.at[src * 2 + k]
        return pltpu.make_async_remote_copy(
            ref, ref, sem, recv_k.at[i, src], device_id=sq(to), device_id_type=MESH)

    def kv_recv(i, land, src):
        kv_copy(i, land, src, (g + 1) % chips, recv_k.at[i, src]).wait_recv()

    def kv_sib(i, land, src, kk):
        ref = land.at[src * 2 + kk]
        return pltpu.make_async_remote_copy(
            ref, ref, send_ks.at[i, src], recv_ks.at[i, src], device_id={"seq": sib}, device_id_type=MESH)

    def kv_own(i, land, what):
        @pl.when(c == 0)
        def _():
            what(kv_copy(i, land, g, base + 1, send_k.at[i, base + 1]))
            what(kv_copy(i, land, g, base + 2, send_k.at[i, base + 2]))

        @pl.when((c == 1) | (c == 2))
        def _():
            what(kv_copy(i, land, g, base + 3, send_k.at[i, base + 3]))

        @pl.loop(base + 4, chips)
        def _(to):
            what(kv_copy(i, land, g, to, send_k.at[i, to]))

    def kv_own_sib(what):
        @pl.when(k == 0)
        def _():
            for i, land in parts:
                what(kv_sib(i, land, g, 0))

    def kv_relay(i, land, src, what):
        @pl.when((c == i + 1) & (src == base))
        def _():
            what(kv_copy(i, land, src, base + 3, send_r.at[i, src]))

        @pl.when((c == 3) & (src == base + 1))
        def _():
            what(kv_copy(i, land, src, base + 2, send_r.at[i, src]))

    dirs = (1, -1)

    def valid(h):
        return (h >= 0) & (h < D)

    with mark("barwait"):
        pl.semaphore_wait(bar, 5 + (chips - 4) + D - 1)

    w_own(lambda cp: cp.start())

    for i, ref in ((0, own_h), (1, row_h)):
        id_copy(i, ref).start()

    kv_own_sib(lambda cp: cp.start())

    step = T // 4 if T % 64 == 0 else T
    steps = [pl.ds(i, step) for i in range(0, T, step)]

    def weigh(ex, values):
        both = jnp.dot(ex.astype(bf), jnp.concatenate([values, jnp.ones_like(values)], axis=1),
                       preferred_element_type=f32)
        return both[:, :HS], both[:, HS:HS + 1]

    qcopy.wait()
    with mark("selfown"):
        for i, rows in enumerate(steps):
            seen = (i + 1) * step
            sc = lax.dot_general(q[rows, :], kall[s, :seen, :], (((1,), (1,)), ((), ())),
                                 preferred_element_type=f32) * scale
            r = lax.broadcasted_iota(jnp.int32, sc.shape, 0) + i * step
            cc = lax.broadcasted_iota(jnp.int32, sc.shape, 1)
            sc = jnp.where(cc <= r, sc, NEG)
            mx = jnp.max(sc, axis=1, keepdims=True)
            m_ref[rows, :] = mx
            acc_ref[rows, :], l_ref[rows, :] = weigh(jnp.exp2(sc - mx), vall[s, :seen, :])

    with mark("cqshift"):
        ccopy.wait()
        shifted = jnp.concatenate([cqr[...].astype(f32), jnp.zeros((tail, HS), f32)], axis=0)
        cqs[d] = pltpu.roll(shifted, 1, 0).astype(bf)
    cq_own(lambda cp: cp.start())

    with mark("wsplit"):
        wcopy.wait()
        w32[...] = wraw[...].astype(f32)
        for kv in range(2):
            wall[d, kv] = w32[pl.ds(kv, wide, stride=2), :].astype(bf)

    def attend(keys, values):
        for rows in steps:
            sc = lax.dot_general(q[rows, :], keys, (((1,), (1,)), ((), ())),
                                 preferred_element_type=f32) * scale
            old = m_ref[rows, :]
            mx = jnp.maximum(old, jnp.max(sc, axis=1, keepdims=True))
            fade = jnp.exp2(old - mx)
            m_ref[rows, :] = mx
            more, total = weigh(jnp.exp2(sc - mx), values)
            l_ref[rows, :] = l_ref[rows, :] * fade + total
            acc_ref[rows, :] = acc_ref[rows, :] * fade + more

    def find(owner_of, row_of):
        row, named = row_of(0), owner_of(0) == d
        for n in range(1, near):
            mine = owner_of(n) == d
            row = jnp.where(mine, row_of(n), row)
            named = named | mine
        return row, named

    def slot_at(j):
        if j == 0:
            return find(lambda n: prev_s[0, n, spans_here - 1], lambda n: prev_s[1, n, spans_here - 1])
        return find(lambda n: own_s[n, j - 1], lambda n: row_s[n, j - 1])

    lane = lax.broadcasted_iota(jnp.int32, (span_len, HS), 1)
    named_ref[...] = jnp.zeros_like(named_ref)

    def pick(j):
        row, named = slot_at(j)
        esel[j * tile_len:(j + 1) * tile_len, :] = encv[row]
        seen = jnp.where(named, 1.0, 0.0)
        named_ref[...] = jnp.where((lane == j) | (lane == half_step + j), seen, named_ref[...])

    per = -(-slots // PARTS)
    chunks = [range(a, min(a + per, slots)) for a in range(0, slots, per)]

    def rows_of(js):
        a = js[0] * span_len
        b = R if js[-1] == slots - 1 else (js[-1] + 1) * span_len
        return slice(a, b)

    def project(h):
        weight = jnp.concatenate([wall[h, 0], wall[h, 1]], axis=1)
        for js in chunks:
            part = pl.ds(js[0] * tile_len, len(js) * tile_len)
            kvs[h, part, :] = jnp.dot(esel[part, :], weight, preferred_element_type=f32).astype(bf)

    def cross(h):
        with mark("attn"):
            blocks = [rows_of([j]) for j in range(slots)]
            sc = jnp.concatenate(
                [lax.dot_general(cqs[h, rows, :], kvs[h, j * tile_len:(j + 1) * tile_len, :HS],
                                 (((1,), (1,)), ((), ())), preferred_element_type=f32)
                 for j, rows in enumerate(blocks)], axis=0) * scale
            mx = jnp.max(sc, axis=1, keepdims=True)
            ex = jnp.exp2(sc - mx)
            tot = []
            for j, rows in enumerate(blocks):
                values = kvs[h, j * tile_len:(j + 1) * tile_len, HS:]
                both = jnp.dot(ex[rows].astype(bf), jnp.concatenate([values, jnp.ones_like(values)], axis=1),
                               preferred_element_type=f32)
                acc_st[h, rows, :] = both[:, :HS]
                tot.append(both[:, HS:])
        with mark("pack"):
            packed = jnp.zeros((span_len, HS), f32)
            for j, rows in enumerate(blocks):
                top, sums = mx[rows], tot[j]
                n = rows.stop - rows.start
                if n < span_len:
                    top = jnp.concatenate([top, jnp.zeros((span_len - n, 1), f32)], axis=0)
                    sums = jnp.concatenate([sums, jnp.zeros((span_len - n, HS), f32)], axis=0)
                packed = jnp.where(lane == j, top, packed)
                packed = jnp.where(lane == half_step + j, sums, packed)
            packed = jnp.where(named_ref[...] > 0, packed, jnp.where(lane < half_step, NEG, 0.0))
            st[h] = sum(
                [packed[r * tail:(r + 1) * tail] if r == 0
                 else pltpu.roll(packed[r * tail:(r + 1) * tail], r * lane_step, 1) for r in range(groups)])

    def unpack(x):
        return jnp.concatenate(
            [x if r == 0 else pltpu.roll(x, HS - r * lane_step, 1) for r in range(groups)], axis=0)

    hops = [range(a, min(a + -(-slots // HOPS), slots)) for a in range(0, slots, -(-slots // HOPS))]

    def ret_copy(h, ch, slot, to):
        a = rows_of(hops[ch])
        part = pl.ds(a.start, a.stop - a.start)
        return pltpu.make_async_remote_copy(
            rout.at[h, part], rin.at[slot, part], sra.at[h, ch], rra.at[slot, ch],
            device_id={"dp": to}, device_id_type=MESH)

    def st_copy(h, slot, to):
        return pltpu.make_async_remote_copy(
            st.at[h], rin_st.at[slot], srs.at[h], rrs.at[slot],
            device_id={"dp": to}, device_id_type=MESH)

    def nearer(h):
        return (h // 2 != pair) & (entry(pair, h // 2) == h)

    def relays(h):
        return nearer(h) & (entry(h // 2, pair) == d)

    def way(h):
        over = nearer(h) & (entry(h // 2, pair) != d)
        return jnp.where(over, D + h, d), jnp.where(over, mate, h)


    packed_lane = lax.broadcasted_iota(jnp.int32, (tail, HS), 1) % lane_step

    def ship(h):
        slot, to = way(h)
        st_copy(h, slot, to).start()
        for ch, js in enumerate(hops):
            rows = rows_of(js)
            rout[h, rows, :] = acc_st[h, rows, :].astype(bf)
            ret_copy(h, ch, slot, to).start()

    def merge(h, slot):
        st_copy(h, slot, mate).wait_recv()
        a, b = st[h], rin_st[slot]
        top = jnp.maximum(a, b)
        fade_a, fade_b = jnp.exp2(a - top), jnp.exp2(b - top)
        tot = (fade_a * pltpu.roll(a, HS - half_step, 1)
               + fade_b * pltpu.roll(b, HS - half_step, 1))
        st[h] = jnp.where(packed_lane < half_step, top, pltpu.roll(tot, half_step, 1))
        fa[...] = unpack(fade_a)
        fb[...] = unpack(fade_b)
        for ch, js in enumerate(hops):
            ret_copy(h, ch, slot, mate).wait_recv()
            for j in js:
                rows = rows_of([j])
                n = rows.stop - rows.start
                acc_st[h, rows, :] = (fa[:n, j:j + 1] * acc_st[h, rows, :]
                                      + fb[:n, j:j + 1] * rin[slot, rows, :].astype(f32))

    def kv_stage(src, i, land):
        kv_recv(i, land, src)
        kv_relay(i, land, src, lambda cp: cp.start())
        kv_sib(i, land, src, k).start()

    def kv_done(src):
        for i, land in parts:
            kv_sib(i, land, src, 1 - k).wait_recv()
        attend(kall[pl.ds(src * 2, 2)].reshape(2 * T, HS), vall[pl.ds(src * 2, 2)].reshape(2 * T, HS))

    def order(i):
        return base + jnp.where(c == 3, (i + 1) % 3, i)

    def z_recv(e):
        for dirn in dirs:
            h = d - dirn * e

            @pl.when(valid(h))
            def _():
                with mark("wz"):
                    w_recv(h, c)

                    @pl.when(passes(h))
                    def _():
                        w_pass(h).start()

                    for cp in w_plane(h):
                        cp.start()
                    w_sib(h, c, k).start()

    def plane_recv(e):
        for dirn in dirs:
            h = d - dirn * e

            @pl.when(valid(h))
            def _():
                with mark("wplane"):
                    for cc in (xc, yc, dc):
                        w_recv(h, cc)
                        w_sib(h, cc, k).start()

    def cq_enter(e):
        for dirn in dirs:
            h = d - dirn * e

            @pl.when(valid(h) & passes(h))
            def _():
                with mark("cqpass"):
                    cq_pass(h).wait_recv()
                    cq_pass(h).start()

    def each_side(e, what):
        @pl.loop(0, 2)
        def _(side):
            h = d + (2 * side - 1) * e

            @pl.when(valid(h))
            def _():
                what(h)

    def prepare(h):
        with mark("wsib"):
            for cc in range(4):
                w_sib(h, cc, 1 - k).wait_recv()
        with mark("proj"):
            project(h)

    edge = (d == 0) | (d == D - 1)

    def answer(h):
        @pl.when(jnp.logical_not(passes(h)))
        def _():
            with mark("cqwait"):
                cq_pass(h).wait_recv()

        cross(h)

        @pl.when(jnp.logical_not(relays(h) | (edge & (h == mate))))
        def _():
            ship(h)

    with mark("gather"):
        ecopy.wait()
        for j in range(1, slots):
            pick(j)

    z_recv(1)

    with mark("ids"):
        for i, ref in ((0, own_h), (1, row_h)):
            id_copy(i, ref).wait_recv()
            pltpu.make_async_copy(prev_v.at[i], prev_s.at[i], id_sem.at[i]).start()
        for i in range(2):
            pltpu.make_async_copy(prev_v.at[i], prev_s.at[i], id_sem.at[i]).wait()
        pick(0)
    with mark("projown"):
        project(d)
    pl.loop(2, D)(z_recv)
    cross(d)

    @pl.when(k == 1)
    def _():
        with mark("selfsib"):
            for i, land in parts:
                kv_sib(i, land, g, 0).wait_recv()
            attend(kall[s - 1], vall[s - 1])

    near_by = jnp.where(c > 2, 2, jnp.where(c > 0, 1, 0))

    pl.loop(1, D)(cq_enter)
    plane_recv(1)
    for i, land in parts:
        kv_own(i, land, lambda cp: cp.start())

    @pl.loop(2, D + 1)
    def _(e):
        @pl.when(e == D)
        def _():
            @pl.loop(0, near_by)
            def _(i):
                with mark("kstage"):
                    kv_stage(order(i), *parts[0])

        each_side(e - 1, prepare)

        @pl.when(e < D)
        def _():
            plane_recv(e)

        each_side(e - 1, answer)

    @pl.loop(0, base)
    def _(src):
        for i, land in parts:
            kv_stage(src, i, land)
        kv_done(src)

    @pl.when(edge)
    def _():
        ship(mate)

    @pl.loop(0, near_by)
    def _(i):
        with mark("vstage"):
            kv_stage(order(i), *parts[1])

    @pl.loop(1, D)
    def _(o):
        h = (d + o) % D

        @pl.when(relays(h))
        def _():
            with mark("relay"):
                merge(h, D + h)
                ship(h)

    def kv_turn(i):
        @pl.when(i < near_by)
        def _():
            with mark("kvdone"):
                kv_done(order(i))

    kv_turn(0)
    kv_turn(1)

    @pl.loop(near_by, c)
    def _(i):
        with mark("laststage"):
            for j, land in parts:
                kv_stage(order(i), j, land)

    @pl.loop(near_by, c)
    def _(i):
        with mark("kvdone"):
            kv_done(order(i))

    with mark("finishatt"):
        att_v[...] = (acc_ref[...] / l_ref[...]).astype(bf)
        acopy = pltpu.make_async_copy(att_v, both_h.at[0], lsem.at[0])
        acopy.start()

    with mark("drain"):
        for i, ref in ((0, own_h), (1, row_h)):
            id_copy(i, ref).wait_send()

        w_own(lambda cp: cp.wait_send())
        cq_own(lambda cp: cp.wait_send())

        @pl.loop(1, D)
        def _(o):
            h = (d + o) % D

            @pl.when(passes(h))
            def _():
                cq_pass(h).wait_send()
                w_pass(h).wait_send()

            for cp in w_plane(h):
                cp.wait_send()
            for cc in range(4):
                w_sib(h, cc, k).wait_send()

        for i, land in parts:
            kv_own(i, land, lambda cp: cp.wait_send())
        kv_own_sib(lambda cp: cp.wait_send())

        @pl.loop(0, g)
        def _(src):
            for i, land in parts:
                kv_relay(i, land, src, lambda cp: cp.wait_send())
                kv_sib(i, land, src, k).wait_send()


    merge(d, mate)

    @pl.loop(1, pairs)
    def _(o):
        there = (pair + o) % pairs
        close = entry(pair, there)

        with mark("mergelast"):
            merge(d, close)

        @pl.when(entry(there, pair) != d)
        def _():
            with mark("mergelast"):
                merge(d, 4 * there + 1 - close)

    with mark("finish"):
        tots = unpack(pltpu.roll(st[d], HS - half_step, 1))
        for j in range(slots):
            rows = rows_of([j])
            n = rows.stop - rows.start
            out = acc_st[d, rows, :] / tots[:n, j:j + 1]
            if j == 0:
                out = jnp.where(s > 0, out, 0.0)
            acc_st[d, rows, :] = out
        crs_v[...] = pltpu.roll(acc_st[d], R - 1, 0)[:T].astype(bf)
        ccopy = pltpu.make_async_copy(crs_v, both_h.at[1], lsem.at[1])
        ccopy.start()


    @pl.loop(1, D)
    def _(o):
        h = (d + o) % D
        st_copy(h, d, mate).wait_send()
        for ch in range(len(hops)):
            ret_copy(h, ch, d, mate).wait_send()

    acopy.wait()
    ccopy.wait()


def on_device(queries, keys, values, cross_queries, encoded, cross_kv_weight, owners, tile_rows):
    S, D = lax.axis_size("seq"), lax.axis_size("dp")
    T, width = queries.shape
    pool_here, tile_len, wide = encoded.shape
    spans_here = owners.shape[0]
    slots = spans_here + 1
    span_len = T // spans_here
    R = T + 16
    w = cross_kv_weight.reshape(2 * wide, HS)
    own, row = owners.T, tile_rows.T
    near = own.shape[0]
    chips = S // 2
    bf, f32 = jnp.bfloat16, jnp.float32
    hbm = pl.BlockSpec(memory_space=pl.ANY)
    dma = pltpu.SemaphoreType.DMA
    both = pl.pallas_call(
        functools.partial(kernel, S, D, 1.0 / math.sqrt(HS)),
        name="retro",
        out_shape=jax.ShapeDtypeStruct((2, T, width), bf),
        in_specs=[pl.BlockSpec(memory_space=pltpu.SMEM)] * 2 + [hbm] * 8,
        out_specs=hbm,
        scratch_shapes=[
            pltpu.VMEM((T, HS), bf),
            pltpu.VMEM((T, HS), bf),
            pltpu.VMEM((2, near, spans_here), jnp.int32),
            pltpu.SMEM((2, near, spans_here), jnp.int32),
            pltpu.VMEM((T, HS), bf),
            pltpu.VMEM((T, HS), bf),
            pltpu.VMEM((wide // 2, HS), bf),
            pltpu.VMEM((wide // 4, HS), bf),
            pltpu.VMEM((2 * wide, HS), bf),
            pltpu.VMEM((2 * wide, HS), f32),
            pltpu.VMEM((pool_here, tile_len, wide), bf),
            pltpu.VMEM((D, 2, wide, HS), bf),
            pltpu.VMEM((slots * tile_len, wide), bf),
            pltpu.VMEM((D, slots * tile_len, 2 * HS), bf),
            pltpu.VMEM((D, R, HS), bf),
            pltpu.VMEM((D, R, HS), f32),
            pltpu.VMEM((D, 16, HS), f32),
            pltpu.VMEM((2 * D, R, HS), bf),
            pltpu.VMEM((2 * D, 16, HS), f32),
            pltpu.VMEM((D, R, HS), bf),
            pltpu.VMEM((span_len, HS), f32),
            pltpu.VMEM((span_len, HS), f32),
            pltpu.VMEM((span_len, HS), f32),
            pltpu.VMEM((S, T, HS), bf),
            pltpu.VMEM((S, T, HS), bf),
            pltpu.VMEM((T, 1), f32),
            pltpu.VMEM((T, 1), f32),
            pltpu.VMEM((T, HS), f32),
            dma((7,)), dma((2,)), dma((2,)), dma((2,)),
            dma((D // 2,)), dma((D,)), dma((D, 3)), dma((D, 4)), dma((D, 4)), dma((D, 4)), dma((D // 2,)), dma((D,)), dma((D,)),
            dma((D, HOPS)), dma((2 * D, HOPS)), dma((D,)), dma((2 * D,)),
            dma((2, chips)), dma((2, chips)), dma((2, chips)), dma((2, chips)), dma((2, chips)),
        ],
        compiler_params=pltpu.CompilerParams(
            collective_id=0, has_side_effects=True, vmem_limit_bytes=60 * 1024 * 1024),
    )(own, row, own, row, queries, keys, values, cross_queries, encoded, w)
    return both[0], both[1]


def solution(mesh):
    placed = (
        P("seq", "dp"),
        P("seq", "dp"),
        P("seq", "dp"),
        P("seq", "dp"),
        P("dp", None, None),
        P(None, None, "dp"),
        P("seq", None),
        P("seq", None),
    )
    return jax.shard_map(
        on_device,
        mesh=mesh,
        in_specs=placed,
        out_specs=(P("seq", "dp"), P("seq", "dp")),
        check_vma=False,
    )
```

```python
import contextlib
import functools
import math

import jax
import jax.numpy as jnp
from jax import lax
from jax.experimental import pallas as pl
from jax.experimental.pallas import tpu as pltpu
from jax.sharding import PartitionSpec as P

HS = 128
NEG = -1e30
LOG2E = math.log2(math.e)
MESH = pl.DeviceIdType.MESH
PARTS = 3
HOPS = 1


def mark(name):
    return contextlib.nullcontext()


def kernel(
    S, D, inv_root,
    own_s, row_s, own_h, row_h, q_h, key_h, val_h, cq_h, enc_h, w_h,
    both_h,
    att_v, crs_v, prev_v, prev_s, q, cqr, wpart, wsend, wraw, w32, encv, wall, esel, kvs, cqs,
    acc_st, st, rin, rin_st, rout, fa, fb, named_ref,
    kall, vall, m_ref, l_ref, acc_ref,
    lsem, id_send, id_recv, id_sem,
    sz, szp, sw, rz, rp, sws, rws, scq, scp, rcq, sra, rra, srs, rrs,
    send_k, recv_k, send_r, send_ks, recv_ks,
):
    f32, bf = jnp.float32, jnp.bfloat16
    s = lax.axis_index("seq")
    d = lax.axis_index("dp")
    k = s % 2
    g = s // 2
    c = g % 4
    base = g - c
    chips = S // 2
    sib = s + 1 - 2 * k
    nxt = (s + 1) % S
    prv = (s + S - 1) % S
    T = q.shape[0]
    near, spans_here = own_s.shape
    slots = spans_here + 1
    span_len = T // spans_here
    tile_len = encv.shape[1]
    wide = encv.shape[2]
    quarter = wide // 4
    R = cqs.shape[1]
    tail = R - T
    groups = span_len // tail
    lane_step = HS // groups
    half_step = lane_step // 2
    scale = inv_root * LOG2E

    def sq(chip):
        return {"seq": chip * 2 + k}

    mine = pl.ds(2 * quarter * c, 2 * quarter)
    wfirst = pltpu.make_async_copy(w_h.at[mine], wpart, lsem.at[6])
    wfirst.start()
    wcopy = pltpu.make_async_copy(w_h, wraw, lsem.at[0])
    kcopy = pltpu.make_async_copy(key_h, kall.at[s], lsem.at[1])
    vcopy = pltpu.make_async_copy(val_h, vall.at[s], lsem.at[2])
    ccopy = pltpu.make_async_copy(cq_h, cqr, lsem.at[3])
    qcopy = pltpu.make_async_copy(q_h, q, lsem.at[4])
    ecopy = pltpu.make_async_copy(enc_h, encv, lsem.at[5])
    for cp in (kcopy, vcopy, qcopy):
        cp.start()

    bar = pltpu.get_barrier_semaphore()

    def greet(to):
        pl.semaphore_signal(bar, 1, device_id=to, device_id_type=MESH)

    greet({"seq": sib})
    greet(sq(base + (c + 1 - 2 * (c % 2))))
    greet(sq(base + (c + 2) % 4))

    @pl.when(k == 1)
    def _():
        greet({"seq": nxt})

    @pl.when(k == 0)
    def _():
        greet({"seq": prv})

    greet(sq(base + 3 - c))

    @pl.loop(1, D)
    def _(o):
        greet({"dp": (d + o) % D})

    @pl.loop(4, chips)
    def _(o):
        greet(sq((base + o) % chips))

    for cp in (ccopy, wcopy, ecopy):
        cp.start()

    with mark("prep"):
        kcopy.wait()
        vcopy.wait()
        wfirst.wait()
        w32[:2 * quarter, :] = wpart[...].astype(f32)
        wsend[...] = w32[pl.ds(k, quarter, stride=2), :].astype(bf)

    def id_copy(i, ref):
        return pltpu.make_async_remote_copy(
            ref, prev_v.at[i], id_send.at[i], id_recv.at[i], device_id={"seq": nxt}, device_id_type=MESH)

    def w_copy(h, to, sem, land):
        ref = wall.at[h, k, pl.ds(c * quarter, quarter)]
        return pltpu.make_async_remote_copy(ref, ref, sem, land.at[h], device_id=to, device_id_type=MESH)

    xc = c + 1 - 2 * (c % 2)
    yc = (c + 2) % 4
    dc = 3 - c

    def w_plane(h):
        return [w_copy(h, sq(base + cc), sw.at[h], rp) for cc in (xc, yc, dc)]

    def w_three(h):
        ref = wall.at[h, k, pl.ds(0, 3 * quarter)]
        return pltpu.make_async_remote_copy(
            ref, ref, sw.at[h], rp.at[h], device_id={"seq": sib}, device_id_type=MESH)

    def w_sib(h, cc):
        ref = wall.at[h, k, pl.ds(cc * quarter, quarter)]
        return pltpu.make_async_remote_copy(
            ref, ref, sws.at[h], rws.at[h], device_id={"seq": sib}, device_id_type=MESH)

    def w_whole(h, kk):
        ref = wall.at[h, kk]
        return pltpu.make_async_remote_copy(
            ref, ref, sws.at[h], rws.at[h], device_id={"seq": sib}, device_id_type=MESH)

    pair = d // 2
    pairs = D // 2
    mate = d + 1 - 2 * (d % 2)

    def entry(other, here):
        return jnp.where(other < here, 2 * here, 2 * here + 1)

    def cq_copy(h, to, sem):
        return pltpu.make_async_remote_copy(
            cqs.at[h], cqs.at[h], sem, rcq.at[h], device_id={"dp": to}, device_id_type=MESH)

    def cq_own(what):
        @pl.loop(0, pairs)
        def _(o):
            there = (pair + o) % pairs
            what(cq_copy(d, jnp.where(o == 0, mate, entry(pair, there)), scq.at[there]))

    def w_own(what):
        @pl.loop(0, pairs)
        def _(o):
            there = (pair + o) % pairs
            what(pltpu.make_async_remote_copy(
                wsend, wall.at[d, k, pl.ds(c * quarter, quarter)], sz.at[there], rz.at[d],
                device_id={"dp": jnp.where(o == 0, mate, entry(pair, there))}, device_id_type=MESH))

    def w_pass(h):
        return w_copy(h, {"dp": mate}, szp.at[h], rz)

    def cq_pass(h):
        return cq_copy(h, mate, scp.at[h])

    def passes(h):
        return (h // 2 != pair) & (entry(h // 2, pair) == d)

    parts = ((0, kall), (1, vall))

    def kv_copy(i, land, src, to, sem):
        ref = land.at[src * 2 + k]
        return pltpu.make_async_remote_copy(
            ref, ref, sem, recv_k.at[i, src], device_id=sq(to), device_id_type=MESH)

    def kv_recv(i, land, src):
        kv_copy(i, land, src, (g + 1) % chips, recv_k.at[i, src]).wait_recv()

    def kv_sib(i, land, src, kk):
        ref = land.at[src * 2 + kk]
        return pltpu.make_async_remote_copy(
            ref, ref, send_ks.at[src], recv_ks.at[src], device_id={"seq": sib}, device_id_type=MESH)

    def kv_both(src):
        ref = kall.at[pl.ds(0, 2)]
        return pltpu.make_async_remote_copy(
            ref, ref, send_ks.at[src], recv_ks.at[src], device_id={"seq": sib}, device_id_type=MESH)

    def kv_own(i, land, what):
        @pl.when(c == 0)
        def _():
            what(kv_copy(i, land, g, base + 1, send_k.at[i, base + 1]))
            what(kv_copy(i, land, g, base + 2, send_k.at[i, base + 2]))

        @pl.when((c == 1) | (c == 2))
        def _():
            what(kv_copy(i, land, g, base + 3, send_k.at[i, base + 3]))

        @pl.loop(base + 4, chips)
        def _(to):
            what(kv_copy(i, land, g, to, send_k.at[i, to]))

    def kv_own_sib(what):
        @pl.when(k == 0)
        def _():
            for i, land in parts:
                what(kv_sib(i, land, g, 0))

    def kv_relay(i, land, src, what):
        @pl.when((c == i + 1) & (src == base))
        def _():
            what(kv_copy(i, land, src, base + 3, send_r.at[i]))

        @pl.when((c == 3) & (src == base + 1))
        def _():
            what(kv_copy(i, land, src, base + 2, send_r.at[i]))

    dirs = (1, -1)

    def valid(h):
        return (h >= 0) & (h < D)

    with mark("barwait"):
        pl.semaphore_wait(bar, 5 + (chips - 4) + D - 1)

    w_own(lambda cp: cp.start())

    for i, ref in ((0, own_h), (1, row_h)):
        id_copy(i, ref).start()

    kv_own_sib(lambda cp: cp.start())

    step = T // 4 if T % 64 == 0 else T
    steps = [pl.ds(i, step) for i in range(0, T, step)]

    def weigh(ex, values):
        both = jnp.dot(ex.astype(bf), jnp.concatenate([values, jnp.ones_like(values)], axis=1),
                       preferred_element_type=f32)
        return both[:, :HS], both[:, HS:HS + 1]

    qcopy.wait()
    with mark("selfown"):
        for i, rows in enumerate(steps):
            seen = (i + 1) * step
            sc = lax.dot_general(q[rows, :], kall[s, :seen, :], (((1,), (1,)), ((), ())),
                                 preferred_element_type=f32) * scale
            r = lax.broadcasted_iota(jnp.int32, sc.shape, 0) + i * step
            cc = lax.broadcasted_iota(jnp.int32, sc.shape, 1)
            sc = jnp.where(cc <= r, sc, NEG)
            mx = jnp.max(sc, axis=1, keepdims=True)
            m_ref[rows, :] = mx
            acc_ref[rows, :], l_ref[rows, :] = weigh(jnp.exp2(sc - mx), vall[s, :seen, :])

    with mark("cqshift"):
        ccopy.wait()
        shifted = jnp.concatenate([cqr[...].astype(f32), jnp.zeros((tail, HS), f32)], axis=0)
        cqs[d] = pltpu.roll(shifted, 1, 0).astype(bf)
    cq_own(lambda cp: cp.start())

    with mark("wsplit"):
        wcopy.wait()
        w32[...] = wraw[...].astype(f32)
        for kv in range(2):
            wall[d, kv] = w32[pl.ds(kv, wide, stride=2), :].astype(bf)

    def attend(keys, values):
        for rows in steps:
            sc = lax.dot_general(q[rows, :], keys, (((1,), (1,)), ((), ())),
                                 preferred_element_type=f32) * scale
            old = m_ref[rows, :]
            mx = jnp.maximum(old, jnp.max(sc, axis=1, keepdims=True))
            fade = jnp.exp2(old - mx)
            m_ref[rows, :] = mx
            more, total = weigh(jnp.exp2(sc - mx), values)
            l_ref[rows, :] = l_ref[rows, :] * fade + total
            acc_ref[rows, :] = acc_ref[rows, :] * fade + more

    def find(owner_of, row_of):
        row, named = row_of(0), owner_of(0) == d
        for n in range(1, near):
            mine = owner_of(n) == d
            row = jnp.where(mine, row_of(n), row)
            named = named | mine
        return row, named

    def slot_at(j):
        if j == 0:
            return find(lambda n: prev_s[0, n, spans_here - 1], lambda n: prev_s[1, n, spans_here - 1])
        return find(lambda n: own_s[n, j - 1], lambda n: row_s[n, j - 1])

    lane = lax.broadcasted_iota(jnp.int32, (span_len, HS), 1)
    named_ref[...] = jnp.zeros_like(named_ref)

    def pick(j):
        row, named = slot_at(j)
        esel[j * tile_len:(j + 1) * tile_len, :] = encv[row]
        seen = jnp.where(named, 1.0, 0.0)
        named_ref[...] = jnp.where((lane == j) | (lane == half_step + j), seen, named_ref[...])

    per = -(-slots // PARTS)
    chunks = [range(a, min(a + per, slots)) for a in range(0, slots, per)]

    def rows_of(js):
        a = js[0] * span_len
        b = R if js[-1] == slots - 1 else (js[-1] + 1) * span_len
        return slice(a, b)

    def project(h):
        weight = jnp.concatenate([wall[h, 0], wall[h, 1]], axis=1)
        for js in chunks:
            part = pl.ds(js[0] * tile_len, len(js) * tile_len)
            kvs[h, part, :] = jnp.dot(esel[part, :], weight, preferred_element_type=f32).astype(bf)

    def cross(h):
        with mark("attn"):
            blocks = [rows_of([j]) for j in range(slots)]
            sc = jnp.concatenate(
                [lax.dot_general(cqs[h, rows, :], kvs[h, j * tile_len:(j + 1) * tile_len, :HS],
                                 (((1,), (1,)), ((), ())), preferred_element_type=f32)
                 for j, rows in enumerate(blocks)], axis=0) * scale
            mx = jnp.max(sc, axis=1, keepdims=True)
            ex = jnp.exp2(sc - mx)
            tot = []
            for j, rows in enumerate(blocks):
                values = kvs[h, j * tile_len:(j + 1) * tile_len, HS:]
                both = jnp.dot(ex[rows].astype(bf), jnp.concatenate([values, jnp.ones_like(values)], axis=1),
                               preferred_element_type=f32)
                acc_st[h, rows, :] = both[:, :HS]
                tot.append(both[:, HS:])
        with mark("pack"):
            packed = jnp.zeros((span_len, HS), f32)
            for j, rows in enumerate(blocks):
                top, sums = mx[rows], tot[j]
                n = rows.stop - rows.start
                if n < span_len:
                    top = jnp.concatenate([top, jnp.zeros((span_len - n, 1), f32)], axis=0)
                    sums = jnp.concatenate([sums, jnp.zeros((span_len - n, HS), f32)], axis=0)
                packed = jnp.where(lane == j, top, packed)
                packed = jnp.where(lane == half_step + j, sums, packed)
            packed = jnp.where(named_ref[...] > 0, packed, jnp.where(lane < half_step, NEG, 0.0))
            st[h] = sum(
                [packed[r * tail:(r + 1) * tail] if r == 0
                 else pltpu.roll(packed[r * tail:(r + 1) * tail], r * lane_step, 1) for r in range(groups)])

    def unpack(x):
        return jnp.concatenate(
            [x if r == 0 else pltpu.roll(x, HS - r * lane_step, 1) for r in range(groups)], axis=0)

    hops = [range(a, min(a + -(-slots // HOPS), slots)) for a in range(0, slots, -(-slots // HOPS))]

    def ret_copy(h, ch, slot, to):
        a = rows_of(hops[ch])
        part = pl.ds(a.start, a.stop - a.start)
        return pltpu.make_async_remote_copy(
            rout.at[h, part], rin.at[slot, part], sra.at[h, ch], rra.at[slot, ch],
            device_id={"dp": to}, device_id_type=MESH)

    def st_copy(h, slot, to):
        return pltpu.make_async_remote_copy(
            st.at[h], rin_st.at[slot], srs.at[h], rrs.at[slot],
            device_id={"dp": to}, device_id_type=MESH)

    def nearer(h):
        return (h // 2 != pair) & (entry(pair, h // 2) == h)

    def relays(h):
        return nearer(h) & (entry(h // 2, pair) == d)

    def way(h):
        over = nearer(h) & (entry(h // 2, pair) != d)
        return jnp.where(over, D + h, d), jnp.where(over, mate, h)


    packed_lane = lax.broadcasted_iota(jnp.int32, (tail, HS), 1) % lane_step

    def ship(h):
        slot, to = way(h)
        st_copy(h, slot, to).start()
        for ch, js in enumerate(hops):
            rows = rows_of(js)
            rout[h, rows, :] = acc_st[h, rows, :].astype(bf)
            ret_copy(h, ch, slot, to).start()

    def merge(h, slot):
        st_copy(h, slot, mate).wait_recv()
        a, b = st[h], rin_st[slot]
        top = jnp.maximum(a, b)
        fade_a, fade_b = jnp.exp2(a - top), jnp.exp2(b - top)
        tot = (fade_a * pltpu.roll(a, HS - half_step, 1)
               + fade_b * pltpu.roll(b, HS - half_step, 1))
        st[h] = jnp.where(packed_lane < half_step, top, pltpu.roll(tot, half_step, 1))
        fa[...] = unpack(fade_a)
        fb[...] = unpack(fade_b)
        for ch, js in enumerate(hops):
            ret_copy(h, ch, slot, mate).wait_recv()
            for j in js:
                rows = rows_of([j])
                n = rows.stop - rows.start
                acc_st[h, rows, :] = (fa[:n, j:j + 1] * acc_st[h, rows, :]
                                      + fb[:n, j:j + 1] * rin[slot, rows, :].astype(f32))

    def kv_stage(src, i, land):
        kv_recv(i, land, src)
        kv_relay(i, land, src, lambda cp: cp.start())
        kv_sib(i, land, src, k).start()

    def kv_done(src):
        kv_both(src).wait_recv()
        attend(kall[pl.ds(src * 2, 2)].reshape(2 * T, HS), vall[pl.ds(src * 2, 2)].reshape(2 * T, HS))

    def order(i):
        return base + jnp.where(c == 3, (i + 1) % 3, i)

    def z_recv(e):
        for dirn in dirs:
            h = d - dirn * e

            @pl.when(valid(h))
            def _():
                with mark("wz"):
                    w_pass(h).wait_recv()

                    @pl.when(passes(h))
                    def _():
                        w_pass(h).start()

                    for cp in w_plane(h):
                        cp.start()
                    w_sib(h, c).start()

    def plane_recv(e):
        for dirn in dirs:
            h = d - dirn * e

            @pl.when(valid(h))
            def _():
                with mark("wplane"):
                    w_three(h).wait_recv()
                    for cc in (xc, yc, dc):
                        w_sib(h, cc).start()

    def cq_enter(e):
        for dirn in dirs:
            h = d - dirn * e

            @pl.when(valid(h) & passes(h))
            def _():
                with mark("cqpass"):
                    cq_pass(h).wait_recv()
                    cq_pass(h).start()

    def each_side(e, what):
        @pl.loop(0, 2)
        def _(side):
            h = d + (2 * side - 1) * e

            @pl.when(valid(h))
            def _():
                what(h)

    def prepare(h):
        with mark("wsib"):
            w_whole(h, 1 - k).wait_recv()
        with mark("proj"):
            project(h)

    edge = (d == 0) | (d == D - 1)

    def answer(h):
        @pl.when(jnp.logical_not(passes(h)))
        def _():
            with mark("cqwait"):
                cq_pass(h).wait_recv()

        cross(h)

        @pl.when(jnp.logical_not(relays(h) | (edge & (h == mate))))
        def _():
            ship(h)

    with mark("gather"):
        ecopy.wait()
        for j in range(1, slots):
            pick(j)

    z_recv(1)

    with mark("ids"):
        for i, ref in ((0, own_h), (1, row_h)):
            id_copy(i, ref).wait_recv()
            pltpu.make_async_copy(prev_v.at[i], prev_s.at[i], id_sem.at[i]).start()
        for i in range(2):
            pltpu.make_async_copy(prev_v.at[i], prev_s.at[i], id_sem.at[i]).wait()
        pick(0)
    with mark("projown"):
        project(d)
    pl.loop(2, D)(z_recv)
    cross(d)

    @pl.when(k == 1)
    def _():
        with mark("selfsib"):
            kv_both(g).wait_recv()
            attend(kall[s - 1], vall[s - 1])

    near_by = jnp.where(c > 2, 2, jnp.where(c > 0, 1, 0))

    pl.loop(1, D)(cq_enter)
    plane_recv(1)
    for i, land in parts:
        kv_own(i, land, lambda cp: cp.start())

    @pl.loop(2, D + 1)
    def _(e):
        @pl.when(e == D)
        def _():
            @pl.loop(0, near_by)
            def _(i):
                with mark("kstage"):
                    kv_stage(order(i), *parts[0])

        each_side(e - 1, prepare)

        @pl.when(e < D)
        def _():
            plane_recv(e)

        each_side(e - 1, answer)

    @pl.loop(0, base)
    def _(src):
        for i, land in parts:
            kv_stage(src, i, land)
        kv_done(src)

    @pl.when(edge)
    def _():
        ship(mate)

    @pl.loop(0, near_by)
    def _(i):
        with mark("vstage"):
            kv_stage(order(i), *parts[1])

    @pl.loop(1, D)
    def _(o):
        h = (d + o) % D

        @pl.when(relays(h))
        def _():
            with mark("relay"):
                merge(h, D + h)
                ship(h)

    def kv_turn(i):
        @pl.when(i < near_by)
        def _():
            with mark("kvdone"):
                kv_done(order(i))

    kv_turn(0)
    kv_turn(1)

    @pl.loop(near_by, c)
    def _(i):
        with mark("laststage"):
            for j, land in parts:
                kv_stage(order(i), j, land)

    @pl.loop(near_by, c)
    def _(i):
        with mark("kvdone"):
            kv_done(order(i))

    with mark("finishatt"):
        att_v[...] = (acc_ref[...] / l_ref[...]).astype(bf)
        acopy = pltpu.make_async_copy(att_v, both_h.at[0], lsem.at[0])
        acopy.start()

    with mark("drain"):
        for i, ref in ((0, own_h), (1, row_h)):
            id_copy(i, ref).wait_send()

        w_own(lambda cp: cp.wait_send())
        cq_own(lambda cp: cp.wait_send())

        @pl.loop(1, D)
        def _(o):
            h = (d + o) % D

            @pl.when(passes(h))
            def _():
                cq_pass(h).wait_send()
                w_pass(h).wait_send()

            w_three(h).wait_send()
            w_whole(h, k).wait_send()

        for i, land in parts:
            kv_own(i, land, lambda cp: cp.wait_send())

        @pl.when(k == 0)
        def _():
            kv_both(g).wait_send()

        @pl.loop(0, g)
        def _(src):
            for i, land in parts:
                kv_relay(i, land, src, lambda cp: cp.wait_send())

            kv_both(src).wait_send()


    merge(d, mate)

    @pl.loop(1, pairs)
    def _(o):
        there = (pair + o) % pairs
        close = entry(pair, there)

        with mark("mergelast"):
            merge(d, close)

        @pl.when(entry(there, pair) != d)
        def _():
            with mark("mergelast"):
                merge(d, 4 * there + 1 - close)

    with mark("finish"):
        tots = unpack(pltpu.roll(st[d], HS - half_step, 1))
        for j in range(slots):
            rows = rows_of([j])
            n = rows.stop - rows.start
            out = acc_st[d, rows, :] / tots[:n, j:j + 1]
            if j == 0:
                out = jnp.where(s > 0, out, 0.0)
            acc_st[d, rows, :] = out
        crs_v[...] = pltpu.roll(acc_st[d], R - 1, 0)[:T].astype(bf)
        ccopy = pltpu.make_async_copy(crs_v, both_h.at[1], lsem.at[1])
        ccopy.start()


    @pl.loop(1, D)
    def _(o):
        h = (d + o) % D
        st_copy(h, d, mate).wait_send()
        for ch in range(len(hops)):
            ret_copy(h, ch, d, mate).wait_send()

    acopy.wait()
    ccopy.wait()


def on_device(queries, keys, values, cross_queries, encoded, cross_kv_weight, owners, tile_rows):
    S, D = lax.axis_size("seq"), lax.axis_size("dp")
    T, width = queries.shape
    pool_here, tile_len, wide = encoded.shape
    spans_here = owners.shape[0]
    slots = spans_here + 1
    span_len = T // spans_here
    R = T + 16
    w = cross_kv_weight.reshape(2 * wide, HS)
    own, row = owners.T, tile_rows.T
    near = own.shape[0]
    chips = S // 2
    bf, f32 = jnp.bfloat16, jnp.float32
    hbm = pl.BlockSpec(memory_space=pl.ANY)
    dma = pltpu.SemaphoreType.DMA
    both = pl.pallas_call(
        functools.partial(kernel, S, D, 1.0 / math.sqrt(HS)),
        name="retro",
        out_shape=jax.ShapeDtypeStruct((2, T, width), bf),
        in_specs=[pl.BlockSpec(memory_space=pltpu.SMEM)] * 2 + [hbm] * 8,
        out_specs=hbm,
        scratch_shapes=[
            pltpu.VMEM((T, HS), bf),
            pltpu.VMEM((T, HS), bf),
            pltpu.VMEM((2, near, spans_here), jnp.int32),
            pltpu.SMEM((2, near, spans_here), jnp.int32),
            pltpu.VMEM((T, HS), bf),
            pltpu.VMEM((T, HS), bf),
            pltpu.VMEM((wide // 2, HS), bf),
            pltpu.VMEM((wide // 4, HS), bf),
            pltpu.VMEM((2 * wide, HS), bf),
            pltpu.VMEM((2 * wide, HS), f32),
            pltpu.VMEM((pool_here, tile_len, wide), bf),
            pltpu.VMEM((D, 2, wide, HS), bf),
            pltpu.VMEM((slots * tile_len, wide), bf),
            pltpu.VMEM((D, slots * tile_len, 2 * HS), bf),
            pltpu.VMEM((D, R, HS), bf),
            pltpu.VMEM((D, R, HS), f32),
            pltpu.VMEM((D, 16, HS), f32),
            pltpu.VMEM((2 * D, R, HS), bf),
            pltpu.VMEM((2 * D, 16, HS), f32),
            pltpu.VMEM((D, R, HS), bf),
            pltpu.VMEM((span_len, HS), f32),
            pltpu.VMEM((span_len, HS), f32),
            pltpu.VMEM((span_len, HS), f32),
            pltpu.VMEM((S, T, HS), bf),
            pltpu.VMEM((S, T, HS), bf),
            pltpu.VMEM((T, 1), f32),
            pltpu.VMEM((T, 1), f32),
            pltpu.VMEM((T, HS), f32),
            dma((7,)), dma((2,)), dma((2,)), dma((2,)),
            dma((D // 2,)), dma((D,)), dma((D,)), dma((D,)), dma((D,)), dma((D,)), dma((D,)), dma((D // 2,)), dma((D,)), dma((D,)),
            dma((D, HOPS)), dma((2 * D, HOPS)), dma((D,)), dma((2 * D,)),
            dma((2, chips)), dma((2, chips)), dma((2,)), dma((chips,)), dma((chips,)),
        ],
        compiler_params=pltpu.CompilerParams(
            collective_id=0, has_side_effects=True, vmem_limit_bytes=60 * 1024 * 1024),
    )(own, row, own, row, queries, keys, values, cross_queries, encoded, w)
    return both[0], both[1]


def solution(mesh):
    placed = (
        P("seq", "dp"),
        P("seq", "dp"),
        P("seq", "dp"),
        P("seq", "dp"),
        P("dp", None, None),
        P(None, None, "dp"),
        P("seq", None),
        P("seq", None),
    )
    return jax.shard_map(
        on_device,
        mesh=mesh,
        in_specs=placed,
        out_specs=(P("seq", "dp"), P("seq", "dp")),
        check_vma=False,
    )
```

```python
import contextlib
import functools
import math

import jax
import jax.numpy as jnp
from jax import lax
from jax.experimental import pallas as pl
from jax.experimental.pallas import tpu as pltpu
from jax.sharding import PartitionSpec as P

HS = 128
NEG = -1e30
LOG2E = math.log2(math.e)
MESH = pl.DeviceIdType.MESH
PARTS = 3
HOPS = 1


def mark(name):
    return contextlib.nullcontext()


def kernel(
    S, D, inv_root,
    own_s, row_s, own_h, row_h, q_h, key_h, val_h, cq_h, enc_h, w_h,
    both_h,
    att_v, crs_v, prev_v, prev_s, q, cqr, wpart, wsend, wraw, w32, encv, wall, esel, kvs, cqs,
    acc_st, st, rin, rin_st, rout, fa, fb, named_ref,
    kall, vall, m_ref, l_ref, acc_ref,
    lsem, id_send, id_recv, id_sem,
    sz, szp, sw, rz, rp, sws, rws, scq, scp, rcq, sra, rra, srs, rrs,
    send_k, recv_k, send_r, send_ks, recv_ks,
):
    f32, bf = jnp.float32, jnp.bfloat16
    s = lax.axis_index("seq")
    d = lax.axis_index("dp")
    k = s % 2
    g = s // 2
    c = g % 4
    base = g - c
    chips = S // 2
    sib = s + 1 - 2 * k
    nxt = (s + 1) % S
    prv = (s + S - 1) % S
    T = q.shape[0]
    near, spans_here = own_s.shape
    slots = spans_here + 1
    span_len = T // spans_here
    tile_len = encv.shape[1]
    wide = encv.shape[2]
    quarter = wide // 4
    R = cqs.shape[1]
    tail = R - T
    groups = span_len // tail
    lane_step = HS // groups
    half_step = lane_step // 2
    scale = inv_root * LOG2E

    def sq(chip):
        return {"seq": chip * 2 + k}

    mine = pl.ds(2 * quarter * c, 2 * quarter)
    wfirst = pltpu.make_async_copy(w_h.at[mine], wpart, lsem.at[6])
    wfirst.start()
    wcopy = pltpu.make_async_copy(w_h, wraw, lsem.at[0])
    kcopy = pltpu.make_async_copy(key_h, kall.at[s], lsem.at[1])
    vcopy = pltpu.make_async_copy(val_h, vall.at[s], lsem.at[2])
    ccopy = pltpu.make_async_copy(cq_h, cqr, lsem.at[3])
    qcopy = pltpu.make_async_copy(q_h, q, lsem.at[4])
    ecopy = pltpu.make_async_copy(enc_h, encv, lsem.at[5])
    for cp in (kcopy, vcopy, qcopy):
        cp.start()

    bar = pltpu.get_barrier_semaphore()

    def greet(to):
        pl.semaphore_signal(bar, 1, device_id=to, device_id_type=MESH)

    greet({"seq": sib})
    greet(sq(base + (c + 1 - 2 * (c % 2))))
    greet(sq(base + (c + 2) % 4))

    @pl.when(k == 1)
    def _():
        greet({"seq": nxt})

    @pl.when(k == 0)
    def _():
        greet({"seq": prv})

    greet(sq(base + 3 - c))

    @pl.loop(1, D)
    def _(o):
        greet({"dp": (d + o) % D})

    @pl.loop(4, chips)
    def _(o):
        greet(sq((base + o) % chips))

    for cp in (ccopy, wcopy, ecopy):
        cp.start()

    with mark("prep"):
        kcopy.wait()
        vcopy.wait()
        wfirst.wait()
        w32[:2 * quarter, :] = wpart[...].astype(f32)
        wsend[...] = w32[pl.ds(k, quarter, stride=2), :].astype(bf)

    def id_copy(i, ref):
        return pltpu.make_async_remote_copy(
            ref, prev_v.at[i], id_send.at[i], id_recv.at[i], device_id={"seq": nxt}, device_id_type=MESH)

    def w_copy(h, to, sem, land):
        ref = wall.at[h, k, pl.ds(c * quarter, quarter)]
        return pltpu.make_async_remote_copy(ref, ref, sem, land.at[h], device_id=to, device_id_type=MESH)

    xc = c + 1 - 2 * (c % 2)
    yc = (c + 2) % 4
    dc = 3 - c

    def w_plane(h):
        return [w_copy(h, sq(base + cc), sw.at[h], rp) for cc in (xc, yc, dc)]

    def w_three(h):
        ref = wall.at[h, k, pl.ds(0, 3 * quarter)]
        return pltpu.make_async_remote_copy(
            ref, ref, sw.at[h], rp.at[h], device_id={"seq": sib}, device_id_type=MESH)

    def w_sib(h, cc):
        ref = wall.at[h, k, pl.ds(cc * quarter, quarter)]
        return pltpu.make_async_remote_copy(
            ref, ref, sws.at[h], rws.at[h], device_id={"seq": sib}, device_id_type=MESH)

    def w_whole(h, kk):
        ref = wall.at[h, kk]
        return pltpu.make_async_remote_copy(
            ref, ref, sws.at[h], rws.at[h], device_id={"seq": sib}, device_id_type=MESH)

    pair = d // 2
    pairs = D // 2
    mate = d + 1 - 2 * (d % 2)

    def entry(other, here):
        return jnp.where(other < here, 2 * here, 2 * here + 1)

    def cq_copy(h, to, sem):
        return pltpu.make_async_remote_copy(
            cqs.at[h], cqs.at[h], sem, rcq.at[h], device_id={"dp": to}, device_id_type=MESH)

    def cq_own(what):
        @pl.loop(0, pairs)
        def _(o):
            there = (pair + o) % pairs
            what(cq_copy(d, jnp.where(o == 0, mate, entry(pair, there)), scq.at[there]))

    def w_own(what):
        @pl.loop(0, pairs)
        def _(o):
            there = (pair + o) % pairs
            what(pltpu.make_async_remote_copy(
                wsend, wall.at[d, k, pl.ds(c * quarter, quarter)], sz.at[there], rz.at[d],
                device_id={"dp": jnp.where(o == 0, mate, entry(pair, there))}, device_id_type=MESH))

    def w_pass(h):
        return w_copy(h, {"dp": mate}, szp.at[h], rz)

    def cq_pass(h):
        return cq_copy(h, mate, scp.at[h])

    def passes(h):
        return (h // 2 != pair) & (entry(h // 2, pair) == d)

    parts = ((0, kall), (1, vall))

    def kv_copy(i, land, src, to, sem):
        ref = land.at[src * 2 + k]
        return pltpu.make_async_remote_copy(
            ref, ref, sem, recv_k.at[i, src], device_id=sq(to), device_id_type=MESH)

    def kv_recv(i, land, src):
        kv_copy(i, land, src, (g + 1) % chips, recv_k.at[i, src]).wait_recv()

    def kv_sib(i, land, src, kk):
        ref = land.at[src * 2 + kk]
        return pltpu.make_async_remote_copy(
            ref, ref, send_ks.at[src], recv_ks.at[src], device_id={"seq": sib}, device_id_type=MESH)

    def kv_both(src):
        ref = kall.at[pl.ds(0, 2)]
        return pltpu.make_async_remote_copy(
            ref, ref, send_ks.at[src], recv_ks.at[src], device_id={"seq": sib}, device_id_type=MESH)

    def kv_own(i, land, what):
        @pl.when(c == 0)
        def _():
            what(kv_copy(i, land, g, base + 1, send_k.at[i, base + 1]))
            what(kv_copy(i, land, g, base + 2, send_k.at[i, base + 2]))

        @pl.when((c == 1) | (c == 2))
        def _():
            what(kv_copy(i, land, g, base + 3, send_k.at[i, base + 3]))

        @pl.loop(base + 4, chips)
        def _(to):
            what(kv_copy(i, land, g, to, send_k.at[i, to]))

    def kv_own_sib(what):
        @pl.when(k == 0)
        def _():
            for i, land in parts:
                what(kv_sib(i, land, g, 0))

    def kv_relay(i, land, src, what):
        @pl.when((c == i + 1) & (src == base))
        def _():
            what(kv_copy(i, land, src, base + 3, send_r.at[i]))

        @pl.when((c == 3) & (src == base + 1))
        def _():
            what(kv_copy(i, land, src, base + 2, send_r.at[i]))

    dirs = (1, -1)

    def valid(h):
        return (h >= 0) & (h < D)

    with mark("barwait"):
        pl.semaphore_wait(bar, 5 + (chips - 4) + D - 1)

    w_own(lambda cp: cp.start())

    for i, ref in ((0, own_h), (1, row_h)):
        id_copy(i, ref).start()

    kv_own_sib(lambda cp: cp.start())

    step = T // 4 if T % 64 == 0 else T
    steps = [pl.ds(i, step) for i in range(0, T, step)]

    def weigh(ex, values):
        both = jnp.dot(ex.astype(bf), jnp.concatenate([values, jnp.ones_like(values)], axis=1),
                       preferred_element_type=f32)
        return both[:, :HS], both[:, HS:HS + 1]

    qcopy.wait()
    with mark("selfown"):
        for i, rows in enumerate(steps):
            seen = (i + 1) * step
            sc = lax.dot_general(q[rows, :], kall[s, :seen, :], (((1,), (1,)), ((), ())),
                                 preferred_element_type=f32) * scale
            r = lax.broadcasted_iota(jnp.int32, sc.shape, 0) + i * step
            cc = lax.broadcasted_iota(jnp.int32, sc.shape, 1)
            sc = jnp.where(cc <= r, sc, NEG)
            mx = jnp.max(sc, axis=1, keepdims=True)
            m_ref[rows, :] = mx
            acc_ref[rows, :], l_ref[rows, :] = weigh(jnp.exp2(sc - mx), vall[s, :seen, :])

    with mark("cqshift"):
        ccopy.wait()
        shifted = jnp.concatenate([cqr[...].astype(f32), jnp.zeros((tail, HS), f32)], axis=0)
        cqs[d] = pltpu.roll(shifted, 1, 0).astype(bf)
    cq_own(lambda cp: cp.start())

    with mark("wsplit"):
        wcopy.wait()
        w32[...] = wraw[...].astype(f32)
        for kv in range(2):
            wall[d, kv] = w32[pl.ds(kv, wide, stride=2), :].astype(bf)

    def attend(keys, values):
        for rows in steps:
            sc = lax.dot_general(q[rows, :], keys, (((1,), (1,)), ((), ())),
                                 preferred_element_type=f32) * scale
            old = m_ref[rows, :]
            mx = jnp.maximum(old, jnp.max(sc, axis=1, keepdims=True))
            fade = jnp.exp2(old - mx)
            m_ref[rows, :] = mx
            more, total = weigh(jnp.exp2(sc - mx), values)
            l_ref[rows, :] = l_ref[rows, :] * fade + total
            acc_ref[rows, :] = acc_ref[rows, :] * fade + more

    def find(owner_of, row_of):
        row, named = row_of(0), owner_of(0) == d
        for n in range(1, near):
            mine = owner_of(n) == d
            row = jnp.where(mine, row_of(n), row)
            named = named | mine
        return row, named

    def slot_at(j):
        if j == 0:
            return find(lambda n: prev_s[0, n, spans_here - 1], lambda n: prev_s[1, n, spans_here - 1])
        return find(lambda n: own_s[n, j - 1], lambda n: row_s[n, j - 1])

    lane = lax.broadcasted_iota(jnp.int32, (span_len, HS), 1)
    named_ref[...] = jnp.zeros_like(named_ref)

    def pick(j):
        row, named = slot_at(j)
        esel[j * tile_len:(j + 1) * tile_len, :] = encv[row]
        seen = jnp.where(named, 1.0, 0.0)
        named_ref[...] = jnp.where((lane == j) | (lane == half_step + j), seen, named_ref[...])

    per = -(-slots // PARTS)
    chunks = [range(a, min(a + per, slots)) for a in range(0, slots, per)]

    def rows_of(js):
        a = js[0] * span_len
        b = R if js[-1] == slots - 1 else (js[-1] + 1) * span_len
        return slice(a, b)

    def project(h):
        weight = jnp.concatenate([wall[h, 0], wall[h, 1]], axis=1)
        for js in chunks:
            part = pl.ds(js[0] * tile_len, len(js) * tile_len)
            kvs[h, part, :] = jnp.dot(esel[part, :], weight, preferred_element_type=f32).astype(bf)

    def cross(h):
        with mark("attn"):
            blocks = [rows_of([j]) for j in range(slots)]
            sc = jnp.concatenate(
                [lax.dot_general(cqs[h, rows, :], kvs[h, j * tile_len:(j + 1) * tile_len, :HS],
                                 (((1,), (1,)), ((), ())), preferred_element_type=f32)
                 for j, rows in enumerate(blocks)], axis=0) * scale
            mx = jnp.max(sc, axis=1, keepdims=True)
            ex = jnp.exp2(sc - mx)
            tot = []
            for j, rows in enumerate(blocks):
                values = kvs[h, j * tile_len:(j + 1) * tile_len, HS:]
                both = jnp.dot(ex[rows].astype(bf), jnp.concatenate([values, jnp.ones_like(values)], axis=1),
                               preferred_element_type=f32)
                acc_st[h, rows, :] = both[:, :HS]
                tot.append(both[:, HS:])
        with mark("pack"):
            packed = jnp.zeros((span_len, HS), f32)
            for j, rows in enumerate(blocks):
                top, sums = mx[rows], tot[j]
                n = rows.stop - rows.start
                if n < span_len:
                    top = jnp.concatenate([top, jnp.zeros((span_len - n, 1), f32)], axis=0)
                    sums = jnp.concatenate([sums, jnp.zeros((span_len - n, HS), f32)], axis=0)
                packed = jnp.where(lane == j, top, packed)
                packed = jnp.where(lane == half_step + j, sums, packed)
            packed = jnp.where(named_ref[...] > 0, packed, jnp.where(lane < half_step, NEG, 0.0))
            st[h] = sum(
                [packed[r * tail:(r + 1) * tail] if r == 0
                 else pltpu.roll(packed[r * tail:(r + 1) * tail], r * lane_step, 1) for r in range(groups)])

    def unpack(x):
        return jnp.concatenate(
            [x if r == 0 else pltpu.roll(x, HS - r * lane_step, 1) for r in range(groups)], axis=0)

    hops = [range(a, min(a + -(-slots // HOPS), slots)) for a in range(0, slots, -(-slots // HOPS))]

    def ret_copy(h, ch, slot, to):
        a = rows_of(hops[ch])
        part = pl.ds(a.start, a.stop - a.start)
        return pltpu.make_async_remote_copy(
            rout.at[h, part], rin.at[slot, part], sra.at[h, ch], rra.at[slot, ch],
            device_id={"dp": to}, device_id_type=MESH)

    def st_copy(h, slot, to):
        return pltpu.make_async_remote_copy(
            st.at[h], rin_st.at[slot], srs.at[h], rrs.at[slot],
            device_id={"dp": to}, device_id_type=MESH)

    def nearer(h):
        return (h // 2 != pair) & (entry(pair, h // 2) == h)

    def relays(h):
        return nearer(h) & (entry(h // 2, pair) == d)

    def way(h):
        over = nearer(h) & (entry(h // 2, pair) != d)
        return jnp.where(over, D + h, d), jnp.where(over, mate, h)


    packed_lane = lax.broadcasted_iota(jnp.int32, (tail, HS), 1) % lane_step

    def ship(h):
        slot, to = way(h)
        st_copy(h, slot, to).start()
        for ch, js in enumerate(hops):
            rows = rows_of(js)
            rout[h, rows, :] = acc_st[h, rows, :].astype(bf)
            ret_copy(h, ch, slot, to).start()

    def merge(h, slot):
        st_copy(h, slot, mate).wait_recv()
        a, b = st[h], rin_st[slot]
        top = jnp.maximum(a, b)
        fade_a, fade_b = jnp.exp2(a - top), jnp.exp2(b - top)
        tot = (fade_a * pltpu.roll(a, HS - half_step, 1)
               + fade_b * pltpu.roll(b, HS - half_step, 1))
        st[h] = jnp.where(packed_lane < half_step, top, pltpu.roll(tot, half_step, 1))
        fa[...] = unpack(fade_a)
        fb[...] = unpack(fade_b)
        for ch, js in enumerate(hops):
            ret_copy(h, ch, slot, mate).wait_recv()
            for j in js:
                rows = rows_of([j])
                n = rows.stop - rows.start
                acc_st[h, rows, :] = (fa[:n, j:j + 1] * acc_st[h, rows, :]
                                      + fb[:n, j:j + 1] * rin[slot, rows, :].astype(f32))

    def kv_stage(src, i, land):
        kv_recv(i, land, src)
        kv_relay(i, land, src, lambda cp: cp.start())
        kv_sib(i, land, src, k).start()

    def kv_done(src):
        kv_both(src).wait_recv()
        attend(kall[pl.ds(src * 2, 2)].reshape(2 * T, HS), vall[pl.ds(src * 2, 2)].reshape(2 * T, HS))

    def order(i):
        return base + jnp.where(c == 3, (i + 1) % 3, i)

    def z_recv(e):
        for dirn in dirs:
            h = d - dirn * e

            @pl.when(valid(h))
            def _():
                with mark("wz"):
                    w_pass(h).wait_recv()

                    @pl.when(passes(h))
                    def _():
                        w_pass(h).start()

                    for cp in w_plane(h):
                        cp.start()
                    w_sib(h, c).start()

    def plane_recv(e):
        for dirn in dirs:
            h = d - dirn * e

            @pl.when(valid(h))
            def _():
                with mark("wplane"):
                    w_three(h).wait_recv()
                    for cc in (xc, yc, dc):
                        w_sib(h, cc).start()

    def cq_enter(e):
        for dirn in dirs:
            h = d - dirn * e

            @pl.when(valid(h) & passes(h))
            def _():
                with mark("cqpass"):
                    cq_pass(h).wait_recv()
                    cq_pass(h).start()

    def each_side(e, what):
        @pl.loop(0, 2)
        def _(side):
            h = d + (2 * side - 1) * e

            @pl.when(valid(h))
            def _():
                what(h)

    def prepare(h):
        with mark("wsib"):
            w_whole(h, 1 - k).wait_recv()
        with mark("proj"):
            project(h)

    edge = (d == 0) | (d == D - 1)

    def answer(h):
        @pl.when(jnp.logical_not(passes(h)))
        def _():
            with mark("cqwait"):
                cq_pass(h).wait_recv()

        cross(h)

        @pl.when(jnp.logical_not(relays(h) | (edge & (h == mate))))
        def _():
            ship(h)

    with mark("gather"):
        ecopy.wait()
        for j in range(1, slots):
            pick(j)

    z_recv(1)

    with mark("ids"):
        for i, ref in ((0, own_h), (1, row_h)):
            id_copy(i, ref).wait_recv()
            pltpu.make_async_copy(prev_v.at[i], prev_s.at[i], id_sem.at[i]).start()
        for i in range(2):
            pltpu.make_async_copy(prev_v.at[i], prev_s.at[i], id_sem.at[i]).wait()
        pick(0)
    with mark("projown"):
        project(d)
    pl.loop(2, D)(z_recv)
    cross(d)

    @pl.when(k == 1)
    def _():
        with mark("selfsib"):
            kv_both(g).wait_recv()
            attend(kall[s - 1], vall[s - 1])

    near_by = jnp.where(c > 2, 2, jnp.where(c > 0, 1, 0))

    pl.loop(1, D)(cq_enter)
    plane_recv(1)
    for i, land in parts:
        kv_own(i, land, lambda cp: cp.start())

    @pl.loop(2, D + 1)
    def _(e):
        @pl.when(e == D)
        def _():
            @pl.loop(0, near_by)
            def _(i):
                with mark("kstage"):
                    kv_stage(order(i), *parts[0])

        each_side(e - 1, prepare)

        @pl.when(e < D)
        def _():
            plane_recv(e)

        each_side(e - 1, answer)

    @pl.loop(0, base)
    def _(src):
        for i, land in parts:
            kv_stage(src, i, land)
        kv_done(src)

    @pl.when(edge)
    def _():
        ship(mate)

    @pl.loop(0, near_by)
    def _(i):
        with mark("vstage"):
            kv_stage(order(i), *parts[1])

    @pl.loop(1, D)
    def _(o):
        h = (d + o) % D

        @pl.when(relays(h))
        def _():
            with mark("relay"):
                merge(h, D + h)
                ship(h)

    def kv_turn(i):
        @pl.when(i < near_by)
        def _():
            with mark("kvdone"):
                kv_done(order(i))

    kv_turn(0)
    kv_turn(1)

    @pl.loop(near_by, c)
    def _(i):
        with mark("laststage"):
            for j, land in parts:
                kv_stage(order(i), j, land)

    @pl.loop(near_by, c)
    def _(i):
        with mark("kvdone"):
            kv_done(order(i))

    with mark("finishatt"):
        att_v[...] = (acc_ref[...] / l_ref[...]).astype(bf)
        acopy = pltpu.make_async_copy(att_v, both_h.at[0], lsem.at[0])
        acopy.start()

    with mark("drain"):
        for i, ref in ((0, own_h), (1, row_h)):
            id_copy(i, ref).wait_send()

        w_own(lambda cp: cp.wait_send())
        cq_own(lambda cp: cp.wait_send())

        @pl.loop(1, D)
        def _(o):
            h = (d + o) % D

            @pl.when(passes(h))
            def _():
                cq_pass(h).wait_send()
                w_pass(h).wait_send()

            w_three(h).wait_send()
            w_whole(h, k).wait_send()

        for i, land in parts:
            kv_own(i, land, lambda cp: cp.wait_send())

        @pl.when(k == 0)
        def _():
            kv_both(g).wait_send()

        @pl.loop(0, g)
        def _(src):
            for i, land in parts:
                kv_relay(i, land, src, lambda cp: cp.wait_send())

            kv_both(src).wait_send()


    @pl.loop(1, pairs)
    def _(o):
        there = (pair + o) % pairs
        close = entry(pair, there)

        with mark("mergelast"):
            merge(d, close)

        @pl.when(entry(there, pair) != d)
        def _():
            with mark("mergelast"):
                merge(d, 4 * there + 1 - close)

    merge(d, mate)

    with mark("finish"):
        tots = unpack(pltpu.roll(st[d], HS - half_step, 1))
        for j in range(slots):
            rows = rows_of([j])
            n = rows.stop - rows.start
            out = acc_st[d, rows, :] / tots[:n, j:j + 1]
            if j == 0:
                out = jnp.where(s > 0, out, 0.0)
            acc_st[d, rows, :] = out
        crs_v[...] = pltpu.roll(acc_st[d], R - 1, 0)[:T].astype(bf)
        ccopy = pltpu.make_async_copy(crs_v, both_h.at[1], lsem.at[1])
        ccopy.start()


    @pl.loop(1, D)
    def _(o):
        h = (d + o) % D
        st_copy(h, d, mate).wait_send()
        for ch in range(len(hops)):
            ret_copy(h, ch, d, mate).wait_send()

    acopy.wait()
    ccopy.wait()


def on_device(queries, keys, values, cross_queries, encoded, cross_kv_weight, owners, tile_rows):
    S, D = lax.axis_size("seq"), lax.axis_size("dp")
    T, width = queries.shape
    pool_here, tile_len, wide = encoded.shape
    spans_here = owners.shape[0]
    slots = spans_here + 1
    span_len = T // spans_here
    R = T + 16
    w = cross_kv_weight.reshape(2 * wide, HS)
    own, row = owners.T, tile_rows.T
    near = own.shape[0]
    chips = S // 2
    bf, f32 = jnp.bfloat16, jnp.float32
    hbm = pl.BlockSpec(memory_space=pl.ANY)
    dma = pltpu.SemaphoreType.DMA
    both = pl.pallas_call(
        functools.partial(kernel, S, D, 1.0 / math.sqrt(HS)),
        name="retro",
        out_shape=jax.ShapeDtypeStruct((2, T, width), bf),
        in_specs=[pl.BlockSpec(memory_space=pltpu.SMEM)] * 2 + [hbm] * 8,
        out_specs=hbm,
        scratch_shapes=[
            pltpu.VMEM((T, HS), bf),
            pltpu.VMEM((T, HS), bf),
            pltpu.VMEM((2, near, spans_here), jnp.int32),
            pltpu.SMEM((2, near, spans_here), jnp.int32),
            pltpu.VMEM((T, HS), bf),
            pltpu.VMEM((T, HS), bf),
            pltpu.VMEM((wide // 2, HS), bf),
            pltpu.VMEM((wide // 4, HS), bf),
            pltpu.VMEM((2 * wide, HS), bf),
            pltpu.VMEM((2 * wide, HS), f32),
            pltpu.VMEM((pool_here, tile_len, wide), bf),
            pltpu.VMEM((D, 2, wide, HS), bf),
            pltpu.VMEM((slots * tile_len, wide), bf),
            pltpu.VMEM((D, slots * tile_len, 2 * HS), bf),
            pltpu.VMEM((D, R, HS), bf),
            pltpu.VMEM((D, R, HS), f32),
            pltpu.VMEM((D, 16, HS), f32),
            pltpu.VMEM((2 * D, R, HS), bf),
            pltpu.VMEM((2 * D, 16, HS), f32),
            pltpu.VMEM((D, R, HS), bf),
            pltpu.VMEM((span_len, HS), f32),
            pltpu.VMEM((span_len, HS), f32),
            pltpu.VMEM((span_len, HS), f32),
            pltpu.VMEM((S, T, HS), bf),
            pltpu.VMEM((S, T, HS), bf),
            pltpu.VMEM((T, 1), f32),
            pltpu.VMEM((T, 1), f32),
            pltpu.VMEM((T, HS), f32),
            dma((7,)), dma((2,)), dma((2,)), dma((2,)),
            dma((D // 2,)), dma((D,)), dma((D,)), dma((D,)), dma((D,)), dma((D,)), dma((D,)), dma((D // 2,)), dma((D,)), dma((D,)),
            dma((D, HOPS)), dma((2 * D, HOPS)), dma((D,)), dma((2 * D,)),
            dma((2, chips)), dma((2, chips)), dma((2,)), dma((chips,)), dma((chips,)),
        ],
        compiler_params=pltpu.CompilerParams(
            collective_id=0, has_side_effects=True, vmem_limit_bytes=60 * 1024 * 1024),
    )(own, row, own, row, queries, keys, values, cross_queries, encoded, w)
    return both[0], both[1]


def solution(mesh):
    placed = (
        P("seq", "dp"),
        P("seq", "dp"),
        P("seq", "dp"),
        P("seq", "dp"),
        P("dp", None, None),
        P(None, None, "dp"),
        P("seq", None),
        P("seq", None),
    )
    return jax.shard_map(
        on_device,
        mesh=mesh,
        in_specs=placed,
        out_specs=(P("seq", "dp"), P("seq", "dp")),
        check_vma=False,
    )
```

```python
import contextlib
import functools
import math

import jax
import jax.numpy as jnp
from jax import lax
from jax.experimental import pallas as pl
from jax.experimental.pallas import tpu as pltpu
from jax.sharding import PartitionSpec as P

HS = 128
NEG = -1e30
LOG2E = math.log2(math.e)
MESH = pl.DeviceIdType.MESH
PARTS = 3
HOPS = 1


def mark(name):
    return contextlib.nullcontext()


def kernel(
    S, D, inv_root,
    own_s, row_s, own_h, row_h, q_h, key_h, val_h, cq_h, enc_h, w_h,
    both_h,
    att_v, crs_v, prev_v, prev_s, q, cqr, wpart, wsend, wraw, w32, encv, wall, esel, kvs, cqs,
    acc_st, st, rin, rin_st, rout, fa, fb, named_ref,
    kall, vall, m_ref, l_ref, acc_ref,
    lsem, id_send, id_recv, id_sem,
    sz, szp, sw, rz, rp, sws, rws, scq, scp, rcq, sra, rra, srs, rrs,
    send_k, recv_k, send_r, send_ks, recv_ks,
):
    f32, bf = jnp.float32, jnp.bfloat16
    s = lax.axis_index("seq")
    d = lax.axis_index("dp")
    k = s % 2
    g = s // 2
    c = g % 4
    base = g - c
    chips = S // 2
    sib = s + 1 - 2 * k
    nxt = (s + 1) % S
    prv = (s + S - 1) % S
    T = q.shape[0]
    near, spans_here = own_s.shape
    slots = spans_here + 1
    span_len = T // spans_here
    tile_len = encv.shape[1]
    wide = encv.shape[2]
    quarter = wide // 4
    R = cqs.shape[1]
    tail = R - T
    groups = span_len // tail
    lane_step = HS // groups
    half_step = lane_step // 2
    scale = inv_root * LOG2E

    def sq(chip):
        return {"seq": chip * 2 + k}

    mine = pl.ds(2 * quarter * c, 2 * quarter)
    wfirst = pltpu.make_async_copy(w_h.at[mine], wpart, lsem.at[6])
    wfirst.start()
    wcopy = pltpu.make_async_copy(w_h, wraw, lsem.at[0])
    kcopy = pltpu.make_async_copy(key_h, kall.at[s], lsem.at[1])
    vcopy = pltpu.make_async_copy(val_h, vall.at[s], lsem.at[2])
    ccopy = pltpu.make_async_copy(cq_h, cqr, lsem.at[3])
    qcopy = pltpu.make_async_copy(q_h, q, lsem.at[4])
    ecopy = pltpu.make_async_copy(enc_h, encv, lsem.at[5])
    for cp in (kcopy, vcopy, qcopy):
        cp.start()

    bar = pltpu.get_barrier_semaphore()

    def greet(to):
        pl.semaphore_signal(bar, 1, device_id=to, device_id_type=MESH)

    greet({"seq": sib})
    greet(sq(base + (c + 1 - 2 * (c % 2))))
    greet(sq(base + (c + 2) % 4))

    @pl.when(k == 1)
    def _():
        greet({"seq": nxt})

    @pl.when(k == 0)
    def _():
        greet({"seq": prv})

    greet(sq(base + 3 - c))

    @pl.loop(1, D)
    def _(o):
        greet({"dp": (d + o) % D})

    @pl.loop(4, chips)
    def _(o):
        greet(sq((base + o) % chips))

    for cp in (ccopy, wcopy, ecopy):
        cp.start()

    with mark("prep"):
        kcopy.wait()
        vcopy.wait()
        wfirst.wait()
        w32[:2 * quarter, :] = wpart[...].astype(f32)
        wsend[...] = w32[pl.ds(k, quarter, stride=2), :].astype(bf)

    def id_copy(i, ref):
        return pltpu.make_async_remote_copy(
            ref, prev_v.at[i], id_send.at[i], id_recv.at[i], device_id={"seq": nxt}, device_id_type=MESH)

    def w_copy(h, to, sem, land):
        ref = wall.at[h, k, pl.ds(c * quarter, quarter)]
        return pltpu.make_async_remote_copy(ref, ref, sem, land.at[h], device_id=to, device_id_type=MESH)

    xc = c + 1 - 2 * (c % 2)
    yc = (c + 2) % 4
    dc = 3 - c

    def w_plane(h):
        return [w_copy(h, sq(base + cc), sw.at[h], rp) for cc in (xc, yc, dc)]

    def w_three(h):
        ref = wall.at[h, k, pl.ds(0, 3 * quarter)]
        return pltpu.make_async_remote_copy(
            ref, ref, sw.at[h], rp.at[h], device_id={"seq": sib}, device_id_type=MESH)

    def w_sib(h, cc):
        ref = wall.at[h, k, pl.ds(cc * quarter, quarter)]
        return pltpu.make_async_remote_copy(
            ref, ref, sws.at[h], rws.at[h], device_id={"seq": sib}, device_id_type=MESH)

    def w_whole(h, kk):
        ref = wall.at[h, kk]
        return pltpu.make_async_remote_copy(
            ref, ref, sws.at[h], rws.at[h], device_id={"seq": sib}, device_id_type=MESH)

    pair = d // 2
    pairs = D // 2
    mate = d + 1 - 2 * (d % 2)

    def entry(other, here):
        return jnp.where(other < here, 2 * here, 2 * here + 1)

    def cq_copy(h, to, sem):
        return pltpu.make_async_remote_copy(
            cqs.at[h], cqs.at[h], sem, rcq.at[h], device_id={"dp": to}, device_id_type=MESH)

    def cq_own(what):
        @pl.loop(0, pairs)
        def _(o):
            there = (pair + o) % pairs
            what(cq_copy(d, jnp.where(o == 0, mate, entry(pair, there)), scq.at[there]))

    def w_own(what):
        @pl.loop(0, pairs)
        def _(o):
            there = (pair + o) % pairs
            what(pltpu.make_async_remote_copy(
                wsend, wall.at[d, k, pl.ds(c * quarter, quarter)], sz.at[there], rz.at[d],
                device_id={"dp": jnp.where(o == 0, mate, entry(pair, there))}, device_id_type=MESH))

    def w_pass(h):
        return w_copy(h, {"dp": mate}, szp.at[h], rz)

    def cq_pass(h):
        return cq_copy(h, mate, scp.at[h])

    def passes(h):
        return (h // 2 != pair) & (entry(h // 2, pair) == d)

    parts = ((0, kall), (1, vall))

    def kv_copy(i, land, src, to, sem):
        ref = land.at[src * 2 + k]
        return pltpu.make_async_remote_copy(
            ref, ref, sem, recv_k.at[i, src], device_id=sq(to), device_id_type=MESH)

    def kv_recv(i, land, src):
        kv_copy(i, land, src, (g + 1) % chips, recv_k.at[i, src]).wait_recv()

    def kv_sib(i, land, src, kk):
        ref = land.at[src * 2 + kk]
        return pltpu.make_async_remote_copy(
            ref, ref, send_ks.at[src], recv_ks.at[src], device_id={"seq": sib}, device_id_type=MESH)

    def kv_both(src):
        ref = kall.at[pl.ds(0, 2)]
        return pltpu.make_async_remote_copy(
            ref, ref, send_ks.at[src], recv_ks.at[src], device_id={"seq": sib}, device_id_type=MESH)

    def kv_own(i, land, what):
        @pl.when(c == 0)
        def _():
            what(kv_copy(i, land, g, base + 1, send_k.at[i, base + 1]))
            what(kv_copy(i, land, g, base + 2, send_k.at[i, base + 2]))

        @pl.when((c == 1) | (c == 2))
        def _():
            what(kv_copy(i, land, g, base + 3, send_k.at[i, base + 3]))

        @pl.loop(base + 4, chips)
        def _(to):
            what(kv_copy(i, land, g, to, send_k.at[i, to]))

    def kv_own_sib(what):
        @pl.when(k == 0)
        def _():
            for i, land in parts:
                what(kv_sib(i, land, g, 0))

    def kv_relay(i, land, src, what):
        @pl.when((c == i + 1) & (src == base))
        def _():
            what(kv_copy(i, land, src, base + 3, send_r.at[i]))

        @pl.when((c == 3) & (src == base + 1))
        def _():
            what(kv_copy(i, land, src, base + 2, send_r.at[i]))

    dirs = (1, -1)

    def valid(h):
        return (h >= 0) & (h < D)

    with mark("barwait"):
        pl.semaphore_wait(bar, 5 + (chips - 4) + D - 1)

    w_own(lambda cp: cp.start())

    for i, ref in ((0, own_h), (1, row_h)):
        id_copy(i, ref).start()

    kv_own_sib(lambda cp: cp.start())

    step = T // 4 if T % 64 == 0 else T
    steps = [pl.ds(i, step) for i in range(0, T, step)]

    def weigh(ex, values):
        both = jnp.dot(ex.astype(bf), jnp.concatenate([values, jnp.ones_like(values)], axis=1),
                       preferred_element_type=f32)
        return both[:, :HS], both[:, HS:HS + 1]

    qcopy.wait()
    with mark("selfown"):
        for i, rows in enumerate(steps):
            seen = (i + 1) * step
            sc = lax.dot_general(q[rows, :], kall[s, :seen, :], (((1,), (1,)), ((), ())),
                                 preferred_element_type=f32) * scale
            r = lax.broadcasted_iota(jnp.int32, sc.shape, 0) + i * step
            cc = lax.broadcasted_iota(jnp.int32, sc.shape, 1)
            sc = jnp.where(cc <= r, sc, NEG)
            mx = jnp.max(sc, axis=1, keepdims=True)
            m_ref[rows, :] = mx
            acc_ref[rows, :], l_ref[rows, :] = weigh(jnp.exp2(sc - mx), vall[s, :seen, :])

    with mark("cqshift"):
        ccopy.wait()
        shifted = jnp.concatenate([cqr[...].astype(f32), jnp.zeros((tail, HS), f32)], axis=0)
        cqs[d] = pltpu.roll(shifted, 1, 0).astype(bf)
    cq_own(lambda cp: cp.start())

    with mark("wsplit"):
        wcopy.wait()
        w32[...] = wraw[...].astype(f32)
        for kv in range(2):
            wall[d, kv] = w32[pl.ds(kv, wide, stride=2), :].astype(bf)

    def attend(keys, values):
        for rows in steps:
            sc = lax.dot_general(q[rows, :], keys, (((1,), (1,)), ((), ())),
                                 preferred_element_type=f32) * scale
            old = m_ref[rows, :]
            mx = jnp.maximum(old, jnp.max(sc, axis=1, keepdims=True))
            fade = jnp.exp2(old - mx)
            m_ref[rows, :] = mx
            more, total = weigh(jnp.exp2(sc - mx), values)
            l_ref[rows, :] = l_ref[rows, :] * fade + total
            acc_ref[rows, :] = acc_ref[rows, :] * fade + more

    def find(owner_of, row_of):
        row, named = row_of(0), owner_of(0) == d
        for n in range(1, near):
            mine = owner_of(n) == d
            row = jnp.where(mine, row_of(n), row)
            named = named | mine
        return row, named

    def slot_at(j):
        if j == 0:
            return find(lambda n: prev_s[0, n, spans_here - 1], lambda n: prev_s[1, n, spans_here - 1])
        return find(lambda n: own_s[n, j - 1], lambda n: row_s[n, j - 1])

    lane = lax.broadcasted_iota(jnp.int32, (span_len, HS), 1)
    named_ref[...] = jnp.zeros_like(named_ref)

    def pick(j):
        row, named = slot_at(j)
        esel[j * tile_len:(j + 1) * tile_len, :] = encv[row]
        seen = jnp.where(named, 1.0, 0.0)
        named_ref[...] = jnp.where((lane == j) | (lane == half_step + j), seen, named_ref[...])

    per = -(-slots // PARTS)
    chunks = [range(a, min(a + per, slots)) for a in range(0, slots, per)]

    def rows_of(js):
        a = js[0] * span_len
        b = R if js[-1] == slots - 1 else (js[-1] + 1) * span_len
        return slice(a, b)

    def project(h):
        weight = jnp.concatenate([wall[h, 0], wall[h, 1]], axis=1)
        for js in chunks:
            part = pl.ds(js[0] * tile_len, len(js) * tile_len)
            kvs[h, part, :] = jnp.dot(esel[part, :], weight, preferred_element_type=f32).astype(bf)

    def cross(h):
        with mark("attn"):
            blocks = [rows_of([j]) for j in range(slots)]
            sc = jnp.concatenate(
                [lax.dot_general(cqs[h, rows, :], kvs[h, j * tile_len:(j + 1) * tile_len, :HS],
                                 (((1,), (1,)), ((), ())), preferred_element_type=f32)
                 for j, rows in enumerate(blocks)], axis=0) * scale
            mx = jnp.max(sc, axis=1, keepdims=True)
            ex = jnp.exp2(sc - mx)
            tot = []
            for j, rows in enumerate(blocks):
                values = kvs[h, j * tile_len:(j + 1) * tile_len, HS:]
                both = jnp.dot(ex[rows].astype(bf), jnp.concatenate([values, jnp.ones_like(values)], axis=1),
                               preferred_element_type=f32)
                acc_st[h, rows, :] = both[:, :HS]
                tot.append(both[:, HS:])
        with mark("pack"):
            packed = jnp.zeros((span_len, HS), f32)
            for j, rows in enumerate(blocks):
                top, sums = mx[rows], tot[j]
                n = rows.stop - rows.start
                if n < span_len:
                    top = jnp.concatenate([top, jnp.zeros((span_len - n, 1), f32)], axis=0)
                    sums = jnp.concatenate([sums, jnp.zeros((span_len - n, HS), f32)], axis=0)
                packed = jnp.where(lane == j, top, packed)
                packed = jnp.where(lane == half_step + j, sums, packed)
            packed = jnp.where(named_ref[...] > 0, packed, jnp.where(lane < half_step, NEG, 0.0))
            st[h] = sum(
                [packed[r * tail:(r + 1) * tail] if r == 0
                 else pltpu.roll(packed[r * tail:(r + 1) * tail], r * lane_step, 1) for r in range(groups)])

    def unpack(x):
        return jnp.concatenate(
            [x if r == 0 else pltpu.roll(x, HS - r * lane_step, 1) for r in range(groups)], axis=0)

    hops = [range(a, min(a + -(-slots // HOPS), slots)) for a in range(0, slots, -(-slots // HOPS))]

    def ret_copy(h, ch, slot, to):
        a = rows_of(hops[ch])
        part = pl.ds(a.start, a.stop - a.start)
        return pltpu.make_async_remote_copy(
            rout.at[h, part], rin.at[slot, part], sra.at[h, ch], rra.at[slot, ch],
            device_id={"dp": to}, device_id_type=MESH)

    def st_copy(h, slot, to):
        return pltpu.make_async_remote_copy(
            st.at[h], rin_st.at[slot], srs.at[h], rrs.at[slot],
            device_id={"dp": to}, device_id_type=MESH)

    def nearer(h):
        return (h // 2 != pair) & (entry(pair, h // 2) == h)

    def relays(h):
        return nearer(h) & (entry(h // 2, pair) == d)

    def way(h):
        over = nearer(h) & (entry(h // 2, pair) != d)
        return jnp.where(over, D + h, d), jnp.where(over, mate, h)


    packed_lane = lax.broadcasted_iota(jnp.int32, (tail, HS), 1) % lane_step

    def ship(h):
        slot, to = way(h)
        st_copy(h, slot, to).start()
        for ch, js in enumerate(hops):
            rows = rows_of(js)
            rout[h, rows, :] = acc_st[h, rows, :].astype(bf)
            ret_copy(h, ch, slot, to).start()

    def merge(h, slot):
        st_copy(h, slot, mate).wait_recv()
        a, b = st[h], rin_st[slot]
        top = jnp.maximum(a, b)
        fade_a, fade_b = jnp.exp2(a - top), jnp.exp2(b - top)
        tot = (fade_a * pltpu.roll(a, HS - half_step, 1)
               + fade_b * pltpu.roll(b, HS - half_step, 1))
        st[h] = jnp.where(packed_lane < half_step, top, pltpu.roll(tot, half_step, 1))
        fa[...] = unpack(fade_a)
        fb[...] = unpack(fade_b)
        for ch, js in enumerate(hops):
            ret_copy(h, ch, slot, mate).wait_recv()
            for j in js:
                rows = rows_of([j])
                n = rows.stop - rows.start
                acc_st[h, rows, :] = (fa[:n, j:j + 1] * acc_st[h, rows, :]
                                      + fb[:n, j:j + 1] * rin[slot, rows, :].astype(f32))

    def kv_stage(src, i, land):
        kv_recv(i, land, src)
        kv_relay(i, land, src, lambda cp: cp.start())
        kv_sib(i, land, src, k).start()

    def kv_done(src):
        kv_both(src).wait_recv()
        attend(kall[pl.ds(src * 2, 2)].reshape(2 * T, HS), vall[pl.ds(src * 2, 2)].reshape(2 * T, HS))

    def order(i):
        return base + jnp.where(c == 3, (i + 1) % 3, i)

    def z_recv(e):
        for dirn in dirs:
            h = d - dirn * e

            @pl.when(valid(h))
            def _():
                with mark("wz"):
                    w_pass(h).wait_recv()

                    @pl.when(passes(h))
                    def _():
                        w_pass(h).start()

                    for cp in w_plane(h):
                        cp.start()
                    w_sib(h, c).start()

    def plane_recv(e):
        for dirn in dirs:
            h = d - dirn * e

            @pl.when(valid(h))
            def _():
                with mark("wplane"):
                    w_three(h).wait_recv()
                    for cc in (xc, yc, dc):
                        w_sib(h, cc).start()

    def cq_enter(e):
        for dirn in dirs:
            h = d - dirn * e

            @pl.when(valid(h) & passes(h))
            def _():
                with mark("cqpass"):
                    cq_pass(h).wait_recv()
                    cq_pass(h).start()

    def each_side(e, what):
        @pl.loop(0, 2)
        def _(side):
            h = d + (2 * side - 1) * e

            @pl.when(valid(h))
            def _():
                what(h)

    def prepare(h):
        with mark("wsib"):
            w_whole(h, 1 - k).wait_recv()
        with mark("proj"):
            project(h)

    edge = (d == 0) | (d == D - 1)

    def answer(h):
        @pl.when(jnp.logical_not(passes(h)))
        def _():
            with mark("cqwait"):
                cq_pass(h).wait_recv()

        cross(h)

        @pl.when(jnp.logical_not(relays(h) | (edge & (h == mate))))
        def _():
            ship(h)

    with mark("gather"):
        ecopy.wait()
        for j in range(1, slots):
            pick(j)

    z_recv(1)
    pl.loop(2, D)(z_recv)

    with mark("ids"):
        for i, ref in ((0, own_h), (1, row_h)):
            id_copy(i, ref).wait_recv()
            pltpu.make_async_copy(prev_v.at[i], prev_s.at[i], id_sem.at[i]).start()
        for i in range(2):
            pltpu.make_async_copy(prev_v.at[i], prev_s.at[i], id_sem.at[i]).wait()
        pick(0)
    with mark("projown"):
        project(d)
    cross(d)

    @pl.when(k == 1)
    def _():
        with mark("selfsib"):
            kv_both(g).wait_recv()
            attend(kall[s - 1], vall[s - 1])

    near_by = jnp.where(c > 2, 2, jnp.where(c > 0, 1, 0))

    pl.loop(1, D)(cq_enter)
    plane_recv(1)
    for i, land in parts:
        kv_own(i, land, lambda cp: cp.start())

    @pl.loop(2, D + 1)
    def _(e):
        @pl.when(e == D)
        def _():
            @pl.loop(0, near_by)
            def _(i):
                with mark("kstage"):
                    kv_stage(order(i), *parts[0])

        each_side(e - 1, prepare)

        @pl.when(e < D)
        def _():
            plane_recv(e)

        each_side(e - 1, answer)

    @pl.loop(0, base)
    def _(src):
        for i, land in parts:
            kv_stage(src, i, land)
        kv_done(src)

    @pl.when(edge)
    def _():
        ship(mate)

    @pl.loop(0, near_by)
    def _(i):
        with mark("vstage"):
            kv_stage(order(i), *parts[1])

    @pl.loop(1, D)
    def _(o):
        h = (d + o) % D

        @pl.when(relays(h))
        def _():
            with mark("relay"):
                merge(h, D + h)
                ship(h)

    def kv_turn(i):
        @pl.when(i < near_by)
        def _():
            with mark("kvdone"):
                kv_done(order(i))

    kv_turn(0)
    kv_turn(1)

    @pl.loop(near_by, c)
    def _(i):
        with mark("laststage"):
            for j, land in parts:
                kv_stage(order(i), j, land)

    @pl.loop(near_by, c)
    def _(i):
        with mark("kvdone"):
            kv_done(order(i))

    with mark("finishatt"):
        att_v[...] = (acc_ref[...] / l_ref[...]).astype(bf)
        acopy = pltpu.make_async_copy(att_v, both_h.at[0], lsem.at[0])
        acopy.start()

    with mark("drain"):
        for i, ref in ((0, own_h), (1, row_h)):
            id_copy(i, ref).wait_send()

        w_own(lambda cp: cp.wait_send())
        cq_own(lambda cp: cp.wait_send())

        @pl.loop(1, D)
        def _(o):
            h = (d + o) % D

            @pl.when(passes(h))
            def _():
                cq_pass(h).wait_send()
                w_pass(h).wait_send()

            w_three(h).wait_send()
            w_whole(h, k).wait_send()

        for i, land in parts:
            kv_own(i, land, lambda cp: cp.wait_send())

        @pl.when(k == 0)
        def _():
            kv_both(g).wait_send()

        @pl.loop(0, g)
        def _(src):
            for i, land in parts:
                kv_relay(i, land, src, lambda cp: cp.wait_send())

            kv_both(src).wait_send()


    @pl.loop(1, pairs)
    def _(o):
        there = (pair + o) % pairs
        close = entry(pair, there)

        with mark("mergelast"):
            merge(d, close)

        @pl.when(entry(there, pair) != d)
        def _():
            with mark("mergelast"):
                merge(d, 4 * there + 1 - close)

    merge(d, mate)

    with mark("finish"):
        tots = unpack(pltpu.roll(st[d], HS - half_step, 1))
        for j in range(slots):
            rows = rows_of([j])
            n = rows.stop - rows.start
            out = acc_st[d, rows, :] / tots[:n, j:j + 1]
            if j == 0:
                out = jnp.where(s > 0, out, 0.0)
            acc_st[d, rows, :] = out
        crs_v[...] = pltpu.roll(acc_st[d], R - 1, 0)[:T].astype(bf)
        ccopy = pltpu.make_async_copy(crs_v, both_h.at[1], lsem.at[1])
        ccopy.start()


    @pl.loop(1, D)
    def _(o):
        h = (d + o) % D
        st_copy(h, d, mate).wait_send()
        for ch in range(len(hops)):
            ret_copy(h, ch, d, mate).wait_send()

    acopy.wait()
    ccopy.wait()


def on_device(queries, keys, values, cross_queries, encoded, cross_kv_weight, owners, tile_rows):
    S, D = lax.axis_size("seq"), lax.axis_size("dp")
    T, width = queries.shape
    pool_here, tile_len, wide = encoded.shape
    spans_here = owners.shape[0]
    slots = spans_here + 1
    span_len = T // spans_here
    R = T + 16
    w = cross_kv_weight.reshape(2 * wide, HS)
    own, row = owners.T, tile_rows.T
    near = own.shape[0]
    chips = S // 2
    bf, f32 = jnp.bfloat16, jnp.float32
    hbm = pl.BlockSpec(memory_space=pl.ANY)
    dma = pltpu.SemaphoreType.DMA
    both = pl.pallas_call(
        functools.partial(kernel, S, D, 1.0 / math.sqrt(HS)),
        name="retro",
        out_shape=jax.ShapeDtypeStruct((2, T, width), bf),
        in_specs=[pl.BlockSpec(memory_space=pltpu.SMEM)] * 2 + [hbm] * 8,
        out_specs=hbm,
        scratch_shapes=[
            pltpu.VMEM((T, HS), bf),
            pltpu.VMEM((T, HS), bf),
            pltpu.VMEM((2, near, spans_here), jnp.int32),
            pltpu.SMEM((2, near, spans_here), jnp.int32),
            pltpu.VMEM((T, HS), bf),
            pltpu.VMEM((T, HS), bf),
            pltpu.VMEM((wide // 2, HS), bf),
            pltpu.VMEM((wide // 4, HS), bf),
            pltpu.VMEM((2 * wide, HS), bf),
            pltpu.VMEM((2 * wide, HS), f32),
            pltpu.VMEM((pool_here, tile_len, wide), bf),
            pltpu.VMEM((D, 2, wide, HS), bf),
            pltpu.VMEM((slots * tile_len, wide), bf),
            pltpu.VMEM((D, slots * tile_len, 2 * HS), bf),
            pltpu.VMEM((D, R, HS), bf),
            pltpu.VMEM((D, R, HS), f32),
            pltpu.VMEM((D, 16, HS), f32),
            pltpu.VMEM((2 * D, R, HS), bf),
            pltpu.VMEM((2 * D, 16, HS), f32),
            pltpu.VMEM((D, R, HS), bf),
            pltpu.VMEM((span_len, HS), f32),
            pltpu.VMEM((span_len, HS), f32),
            pltpu.VMEM((span_len, HS), f32),
            pltpu.VMEM((S, T, HS), bf),
            pltpu.VMEM((S, T, HS), bf),
            pltpu.VMEM((T, 1), f32),
            pltpu.VMEM((T, 1), f32),
            pltpu.VMEM((T, HS), f32),
            dma((7,)), dma((2,)), dma((2,)), dma((2,)),
            dma((D // 2,)), dma((D,)), dma((D,)), dma((D,)), dma((D,)), dma((D,)), dma((D,)), dma((D // 2,)), dma((D,)), dma((D,)),
            dma((D, HOPS)), dma((2 * D, HOPS)), dma((D,)), dma((2 * D,)),
            dma((2, chips)), dma((2, chips)), dma((2,)), dma((chips,)), dma((chips,)),
        ],
        compiler_params=pltpu.CompilerParams(
            collective_id=0, has_side_effects=True, vmem_limit_bytes=60 * 1024 * 1024),
    )(own, row, own, row, queries, keys, values, cross_queries, encoded, w)
    return both[0], both[1]


def solution(mesh):
    placed = (
        P("seq", "dp"),
        P("seq", "dp"),
        P("seq", "dp"),
        P("seq", "dp"),
        P("dp", None, None),
        P(None, None, "dp"),
        P("seq", None),
        P("seq", None),
    )
    return jax.shard_map(
        on_device,
        mesh=mesh,
        in_specs=placed,
        out_specs=(P("seq", "dp"), P("seq", "dp")),
        check_vma=False,
    )
```
